32 devices in a mesh: chain: 32 (over z, y, x, core).
Axes of the slice: x: 2, y: 2, z: 4, core: 2. Of those that a mesh axis runs over, the one named last changes fastest.
Arguments:
- ham: float32 [32, 3, 256, 256], P('chain'), may hold values from -5 to 28, as said below
- pert: float32 [32, 3, 256, 256], P('chain'), may hold values from -2 to 2, as said below
Outputs:
- dens: float32 [32, 3, 256, 256], P('chain')
- response: float32 [32, 3, 256, 256], P('chain')
The draws below stay inside these ranges and needn't reach their ends.
Inputs may be any that keep to these rules, and one draw needn't show every extreme that they name: ham is symmetric: ham[i, 0] is the transpose of ham[i-1, 2] (ham[0, 0] that of ham[31, 2]) and every ham[i, 1] is symmetric. pert is symmetric in the same way.
All inputs are finite; a program needn't handle non-finite values.
Results may differ from the reference program's by a relative error of at most 0.0001.
Values sent between devices are 32-bit elements; how exact they have to be, the bound alone decides.
A program may use at most 64 MiB of HBM per device.

```python
import math
import jax
import jax.numpy as jnp
from jax import lax

BAND = 256
ITERS = 3
NBLK = 32
ROWS = 8192


def symmetric_blocks(key, scale, with_onsite):
    key_upper, key_diag, key_rows, key_hop, key_site = jax.random.split(key, 5)
    upper_noise = jnp.clip(jax.random.normal(key_upper, (NBLK, BAND, BAND)), -4.0, 4.0)
    diag_noise = jnp.clip(jax.random.normal(key_diag, (NBLK, BAND, BAND)), -4.0, 4.0)
    row_scale = jnp.exp(jax.random.uniform(key_rows, (NBLK, BAND), minval=0.0, maxval=0.5 * math.log(10.0)))
    next_scale = jnp.roll(row_scale, -1, axis=0)
    upper_block = scale * upper_noise * (row_scale[:, :, None] * next_scale[:, None, :])
    diag_sym = 0.5 * (diag_noise + jnp.transpose(diag_noise, (0, 2, 1)))
    diag_block = scale * diag_sym * (row_scale[:, :, None] * row_scale[:, None, :])
    if with_onsite:
        eye_block = jnp.eye(BAND, dtype=jnp.float32)
        hopping = jax.random.uniform(key_hop, (NBLK, BAND), minval=1.5, maxval=4.5)
        positions = jnp.arange(NBLK * BAND, dtype=jnp.float32).reshape(NBLK, BAND)
        ramp_level = 5.0 + 10.0 * positions / (NBLK * BAND)
        site_factor = jax.random.uniform(key_site, (NBLK, BAND), minval=0.2, maxval=1.8)
        onsite = ramp_level * site_factor
        upper_block = upper_block - eye_block[None, :, :] * hopping[:, :, None]
        diag_block = diag_block + eye_block[None, :, :] * onsite[:, :, None]
    lower_block = jnp.transpose(jnp.roll(upper_block, 1, axis=0), (0, 2, 1))
    return jnp.stack([lower_block, diag_block, upper_block], axis=1).astype(jnp.float32)


def draw_ham(key, part):
    return symmetric_blocks(jax.random.fold_in(key, 11), 0.006, True)


def draw_pert(key, part):
    return symmetric_blocks(jax.random.fold_in(key, 23), 0.05, False)


def setup_inputs(seed: int = 0) -> dict:
    splits = jax.random.split(jax.random.key(seed), 3)
    return {
        "ham": draw_ham(jax.random.fold_in(splits[2], 71), 0),
        "pert": draw_pert(jax.random.fold_in(splits[2], 71), 0),
    }


def matmul(first, second):
    return jnp.einsum("nij,njk->nik", first, second, precision=lax.Precision.HIGHEST)


def multiply(left, right):
    before = jnp.roll(right, 1, axis=0)
    after = jnp.roll(right, -1, axis=0)
    lower_out = matmul(left[:, 0], before[:, 1]) + matmul(left[:, 1], right[:, 0])
    centre_out = matmul(left[:, 0], before[:, 2]) + matmul(left[:, 1], right[:, 1]) + matmul(left[:, 2], after[:, 0])
    upper_out = matmul(left[:, 1], right[:, 2]) + matmul(left[:, 2], after[:, 1])
    return jnp.stack([lower_out, centre_out, upper_out], axis=1)


def symmetrize(matrix):
    upper_prev = jnp.roll(matrix[:, 2], 1, axis=0)
    lower_next = jnp.roll(matrix[:, 0], -1, axis=0)
    lower = 0.5 * (matrix[:, 0] + jnp.swapaxes(upper_prev, 1, 2))
    centre = 0.5 * (matrix[:, 1] + jnp.swapaxes(matrix[:, 1], 1, 2))
    upper = 0.5 * (matrix[:, 2] + jnp.swapaxes(lower_next, 1, 2))
    return jnp.stack([lower, centre, upper], axis=1)


def reference(ham, pert):
    onsite = jnp.diagonal(ham[:, 1], axis1=1, axis2=2)
    radius = jnp.sum(jnp.abs(ham), axis=(1, 3)) - jnp.abs(onsite)
    centre_energy = jnp.sum(onsite) / ROWS
    top_end = jnp.max(onsite + radius)
    bottom_end = jnp.min(onsite - radius)
    spectral_bound = jnp.maximum(top_end - centre_energy, centre_energy - bottom_end) + 1e-6
    eye_block = jnp.eye(BAND, dtype=jnp.float32)
    identity = jnp.zeros_like(ham).at[:, 1].set(jnp.broadcast_to(eye_block, (ham.shape[0], BAND, BAND)))
    sign_x = (centre_energy * identity - ham) / spectral_bound
    tangent = -pert / spectral_bound
    for step in range(ITERS):
        square = multiply(sign_x, sign_x)
        cube = symmetrize(multiply(square, sign_x))
        mixed = multiply(sign_x, tangent) + multiply(tangent, sign_x)
        chained = symmetrize(multiply(mixed, sign_x) + multiply(square, tangent))
        sign_x, tangent = 1.5 * sign_x - 0.5 * cube, 1.5 * tangent - 0.5 * chained
    dens = 0.5 * (identity - sign_x)
    response = -0.5 * spectral_bound * tangent
    return dens, response
```

```python
import functools

import jax
import jax.numpy as jnp
import numpy as np
from jax import lax
from jax.experimental import pallas as pl
from jax.experimental.pallas import tpu as pltpu
from jax.sharding import PartitionSpec as P

ITERS = 3
F32, BF16 = jnp.float32, jnp.bfloat16
MESH = pl.DeviceIdType.MESH

D, DD = 0, 1
E, DE = (2, 3), (4, 5)
ET, DET = (6, 7), (8, 9)
DN, DDN = (10, 11), (12, 13)
SQ, MX = 14, 15
SQE, MXE = (16, 17), (18, 19)
SQN, MXN = (20, 21), (22, 23)
NEW, NEWT = (24, 25), (26, 27)
SLOTS = 28


def kernel(n, ham_hbm, pert_hbm, dens_ref, resp_ref, ham_ref, pert_ref, split, state, partial,
           outbox, inbox, stat_out, stat_in, load_sem, send_sem, recv_sem, stat_send, stat_recv):
    b = ham_hbm.shape[-1]
    loads = [
        pltpu.make_async_copy(ham_hbm, ham_ref, load_sem.at[0]),
        pltpu.make_async_copy(pert_hbm, pert_ref, load_sem.at[1]),
    ]
    for load in loads:
        load.start()
    h = b // 2
    me = lax.axis_index("chain")
    sides = (lax.rem(me + n - 1, n), lax.rem(me + 1, n))

    barrier = pltpu.get_barrier_semaphore()

    @pl.loop(1, n)
    def _(off):
        pl.semaphore_signal(
            barrier, inc=1, device_id=(lax.rem(me + off, n),), device_id_type=MESH
        )

    row_h = lax.broadcasted_iota(jnp.int32, (h, h), 0)
    col_h = lax.broadcasted_iota(jnp.int32, (h, h), 1)
    row_b = lax.broadcasted_iota(jnp.int32, (b, b), 0)
    col_b = lax.broadcasted_iota(jnp.int32, (b, b), 1)
    eye = row_b == col_b

    def pack(step, kind, which, m):
        corner = m[h:, h:]
        outbox[step, kind, which, 0:h] = m[:h, h:]
        outbox[step, kind, which, h : 2 * h] = jnp.where(row_h <= col_h, m[:h, :h], corner)
        diag = jnp.sum(jnp.where(row_h == col_h, corner, 0.0), axis=0, keepdims=True)
        outbox[step, kind, which, 2 * h : 2 * h + 8] = jnp.broadcast_to(diag, (8, h))

    def unpack(step, kind, side, which):
        off = inbox[step, kind, which, side, 0:h]
        mixed = inbox[step, kind, which, side, h : 2 * h]
        diag = inbox[step, kind, which, side, 2 * h : 2 * h + 1]
        turned = mixed.T
        first = jnp.where(row_h <= col_h, mixed, turned)
        last = jnp.where(row_h > col_h, mixed, jnp.where(row_h == col_h, diag, turned))
        return jnp.concatenate(
            [jnp.concatenate([first, off], axis=1), jnp.concatenate([off.T, last], axis=1)],
            axis=0,
        )

    def copy(step, kind, which, side):
        return pltpu.make_async_remote_copy(
            src_ref=outbox.at[step, kind, which, pl.ds(0, 2 * h + 2)],
            dst_ref=inbox.at[step, kind, which, 1 - side, pl.ds(0, 2 * h + 2)],
            send_sem=send_sem.at[step, kind, which, side],
            recv_sem=recv_sem.at[step, kind, which, 1 - side],
            device_id=(sides[side],),
            device_id_type=MESH,
        )

    def send(step, kind, which):
        for side in (0, 1):
            copy(step, kind, which, side).start()

    def arrived(step, kind, which, side):
        copy(step, kind, which, 1 - side).wait_recv()

    def put(slot, m):
        high = m.astype(BF16)
        split[slot, 0] = high
        split[slot, 1] = (m - high.astype(F32)).astype(BF16)

    def total(*terms):
        left, right = [], []
        for a, c in terms:
            left += [split[a, 0], split[a, 0], split[a, 1]]
            right += [split[c, 0], split[c, 1], split[c, 0]]
        return jnp.dot(
            jnp.concatenate(left, axis=1),
            jnp.concatenate(right, axis=0),
            preferred_element_type=F32,
        )

    def sym(m):
        return 0.5 * (m + m.T)

    def put_edges(slots, turned, values):
        for side in (0, 1):
            put(slots[side], values[side])
            put(turned[side], values[side].T)

    loads[0].wait()
    centre = ham_ref[0, 1]
    onsite = jnp.sum(jnp.where(eye, centre, 0.0), axis=1, keepdims=True)
    reach = jnp.sum(
        jnp.abs(ham_ref[0, 0]) + jnp.abs(centre) + jnp.abs(ham_ref[0, 2]), axis=1, keepdims=True
    ) - jnp.abs(onsite)
    lane = lax.broadcasted_iota(jnp.int32, (1, 128), 1)
    mine = jnp.where(
        lane == 0,
        jnp.sum(onsite, axis=0, keepdims=True),
        jnp.where(
            lane == 1,
            jnp.max(onsite + reach, axis=0, keepdims=True),
            jnp.min(onsite - reach, axis=0, keepdims=True),
        ),
    )
    stat_out[...] = mine
    level = jnp.sum(onsite, axis=0, keepdims=True) / b
    shifted = centre - jnp.where(eye, level, 0.0)
    pack(0, 0, 0, shifted)
    put(D, shifted)
    put_edges(E, ET, (ham_ref[0, 0], ham_ref[0, 2]))
    loads[1].wait()
    pack(0, 0, 1, pert_ref[0, 1])
    outbox[0, 0, 0, 2 * h + 1 : 2 * h + 2] = jnp.broadcast_to(level, (1, h))
    pl.semaphore_wait(barrier, n - 1)

    @pl.loop(1, n)
    def _(off):
        pltpu.make_async_remote_copy(
            src_ref=stat_out,
            dst_ref=stat_in.at[me],
            send_sem=stat_send,
            recv_sem=stat_recv,
            device_id=(lax.rem(me + off, n),),
            device_id_type=MESH,
        ).start()

    send(0, 0, 0)
    send(0, 0, 1)
    stat_in[me] = mine
    put(DD, pert_ref[0, 1])
    put_edges(DE, DET, (pert_ref[0, 0], pert_ref[0, 2]))
    square = total((D, D), (E[0], ET[0]), (E[1], ET[1]))
    pack(0, 1, 0, square)
    send(0, 1, 0)
    mixed = total((D, DD), (E[0], DET[0]), (E[1], DET[1]))
    mixed = mixed + mixed.T
    pack(0, 1, 1, mixed)
    send(0, 1, 1)
    partial[0, 0] = square
    partial[0, 1] = mixed
    everyone = pltpu.make_async_remote_copy(
        src_ref=stat_in.at[pl.ds(0, n - 1)],
        dst_ref=stat_in.at[pl.ds(0, n - 1)],
        send_sem=stat_send,
        recv_sem=stat_recv,
        device_id=(sides[0],),
        device_id_type=MESH,
    )
    everyone.wait_recv()
    everyone.wait_send()
    stats = stat_in[...].reshape(n, 128)
    energy = jnp.sum(stats[:, 0:1], axis=0, keepdims=True) / (n * b)
    top = jnp.max(stats[:, 1:2], axis=0, keepdims=True)
    bottom = jnp.min(stats[:, 2:3], axis=0, keepdims=True)
    bound = jnp.maximum(top - energy, energy - bottom) + 1e-6
    inverse = 1.0 / bound

    def rescale(gap, node, square, dnode, mixed):
        return (
            (jnp.where(eye, gap, 0.0) - node) * inverse,
            (jnp.where(eye, gap * gap, 0.0) - (2.0 * gap) * node + square) * (inverse * inverse),
            (mixed - (2.0 * gap) * dnode) * (inverse * inverse),
        )

    gap = energy - level
    node, square, mixed = rescale(
        gap, ham_ref[0, 1] - jnp.where(eye, level, 0.0), partial[0, 0], pert_ref[0, 1],
        partial[0, 1],
    )
    put(SQ, square)
    put(MX, mixed)
    for k in range(3):
        state[0, k] = node if k == 1 else -ham_ref[0, k] * inverse
        state[1, k] = -pert_ref[0, k] * inverse

    put(D, state[0, 1])
    put(DD, state[1, 1])
    put_edges(E, ET, (state[0, 0], state[0, 2]))
    put_edges(DE, DET, (state[1, 0], state[1, 2]))

    @pl.loop(0, ITERS)
    def _(step):
        for s in (0, 1):
            arrived(step, 0, 0, s)

            @pl.when(step == 0)
            def _():
                gap = energy - inbox[0, 0, 0, s, 2 * h + 1 : 2 * h + 2, 0:1]
                put(DN[s], (jnp.where(eye, gap, 0.0) - unpack(0, 0, s, 0)) * inverse)

            @pl.when(step > 0)
            def _():
                put(DN[s], unpack(step, 0, s, 0))

            put(SQE[s], total((D, E[s]), (E[s], DN[s])))
        state[0, 1] = 1.5 * state[0, 1] - 0.5 * sym(
            total((SQ, D), (SQE[0], ET[0]), (SQE[1], ET[1]))
        )

        @pl.when(step < ITERS - 1)
        def _():
            pack(step + 1, 0, 0, state[0, 1])
            send(step + 1, 0, 0)

        for s in (0, 1):
            arrived(step, 0, 1, s)
            scale = jnp.where(step == 0, -inverse, 1.0)
            put(DDN[s], unpack(step, 0, s, 1) * scale)
            put(MXE[s], total((D, DE[s]), (E[s], DDN[s]), (DD, E[s]), (DE[s], DN[s])))
        state[1, 1] = 1.5 * state[1, 1] - 0.5 * sym(
            total(
                (MX, D), (MXE[0], ET[0]), (MXE[1], ET[1]),
                (SQ, DD), (SQE[0], DET[0]), (SQE[1], DET[1]),
            )
        )

        @pl.when(step < ITERS - 1)
        def _():
            pack(step + 1, 0, 1, state[1, 1])
            send(step + 1, 0, 1)

        for s in (0, 1):
            partial[0, s] = total((SQ, E[s]), (SQE[s], DN[s]), (D, SQE[s]))
            partial[1, s] = total(
                (MX, E[s]), (MXE[s], DN[s]), (SQ, DE[s]), (SQE[s], DDN[s]),
                (D, MXE[s]), (DD, SQE[s]),
            )
        for s in (0, 1):
            arrived(step, 1, 0, s)

            @pl.when(step == 0)
            def _():
                gap = energy - inbox[0, 0, 0, s, 2 * h + 1 : 2 * h + 2, 0:1]
                near = unpack(0, 0, s, 0)
                put(SQN[s], rescale(gap, near, unpack(0, 1, s, 0), near, near)[1])

            @pl.when(step > 0)
            def _():
                put(SQN[s], unpack(step, 1, s, 0))

            state[0, 2 * s] = 1.5 * state[0, 2 * s] - 0.25 * (
                partial[0, s] + total((E[s], SQN[s]))
            )
            partial[1, s] += total((DE[s], SQN[s]))

        @pl.when(step < ITERS - 1)
        def _():
            put(D, state[0, 1])
            put_edges(NEW, NEWT, (state[0, 0], state[0, 2]))
            square = total((D, D), (NEW[0], NEWT[0]), (NEW[1], NEWT[1]))
            put(SQ, square)
            pack(step + 1, 1, 0, square)
            send(step + 1, 1, 0)

        for s in (0, 1):
            arrived(step, 1, 1, s)

            @pl.when(step == 0)
            def _():
                gap = energy - inbox[0, 0, 0, s, 2 * h + 1 : 2 * h + 2, 0:1]
                near, dnear = unpack(0, 0, s, 0), unpack(0, 0, s, 1)
                put(MXN[s], rescale(gap, near, near, dnear, unpack(0, 1, s, 1))[2])

            @pl.when(step > 0)
            def _():
                put(MXN[s], unpack(step, 1, s, 1))

            state[1, 2 * s] = 1.5 * state[1, 2 * s] - 0.25 * (
                partial[1, s] + total((E[s], MXN[s]))
            )

        @pl.when(step < ITERS - 1)
        def _():
            put(DD, state[1, 1])
            put_edges(DE, DET, (state[1, 0], state[1, 2]))
            for side in (0, 1):
                split[E[side]] = split[NEW[side]]
                split[ET[side]] = split[NEWT[side]]
            mixed = total((D, DD), (E[0], DET[0]), (E[1], DET[1]))
            mixed = mixed + mixed.T
            put(MX, mixed)
            pack(step + 1, 1, 1, mixed)
            send(step + 1, 1, 1)

    for k in range(3):
        shift = jnp.where(eye, 0.5, 0.0) if k == 1 else 0.0
        dens_ref[0, k] = shift - 0.5 * state[0, k]
        resp_ref[0, k] = (-0.5 * bound) * state[1, k]
    for step in range(ITERS):
        for kind, which, side in np.ndindex(2, 2, 2):
            copy(step, kind, which, side).wait_send()


def per_device(n, ham, pert):
    b = ham.shape[-1]
    packed = (b + 8, b // 2)
    return pl.pallas_call(
        functools.partial(kernel, n),
        out_shape=(jax.ShapeDtypeStruct(ham.shape, F32), jax.ShapeDtypeStruct(ham.shape, F32)),
        in_specs=[pl.BlockSpec(memory_space=pltpu.HBM)] * 2,
        out_specs=[pl.BlockSpec(memory_space=pltpu.VMEM)] * 2,
        scratch_shapes=[
            pltpu.VMEM(ham.shape, F32),
            pltpu.VMEM(pert.shape, F32),
            pltpu.VMEM((SLOTS, 2, b, b), BF16),
            pltpu.VMEM((2, 3, b, b), F32),
            pltpu.VMEM((2, 2, b, b), F32),
            pltpu.VMEM((ITERS, 2, 2) + packed, F32),
            pltpu.VMEM((ITERS, 2, 2, 2) + packed, F32),
            pltpu.VMEM((1, 128), F32),
            pltpu.VMEM((n, 1, 128), F32),
            pltpu.SemaphoreType.DMA((2,)),
            pltpu.SemaphoreType.DMA((ITERS, 2, 2, 2)),
            pltpu.SemaphoreType.DMA((ITERS, 2, 2, 2)),
            pltpu.SemaphoreType.DMA,
            pltpu.SemaphoreType.DMA,
        ],
        compiler_params=pltpu.CompilerParams(
            collective_id=0, has_side_effects=True, vmem_limit_bytes=52 * 1024 * 1024
        ),
    )(ham, pert)


def solution(mesh):
    n = mesh.shape["chain"]
    spec = P("chain", None, None, None)
    return jax.shard_map(
        functools.partial(per_device, n),
        mesh=mesh,
        in_specs=(spec, spec),
        out_specs=(spec, spec),
        check_vma=False,
    )
```

```python
import functools

import jax
import jax.numpy as jnp
from jax import lax
from jax.experimental import pallas as pl
from jax.experimental.pallas import tpu as pltpu
from jax.sharding import PartitionSpec as P

ITERS = 3
GROUP = 8
F32, BF16 = jnp.float32, jnp.bfloat16
MESH = pl.DeviceIdType.MESH

D, DD = 0, 1
E, DE = (2, 3), (4, 5)
DN, DDN = (6, 7), (8, 9)
AN, DAN = (10, 11), (12, 13)
A, DA, T, DT = 14, 15, 16, 17
F, U, V, W = (18, 19), (20, 21), (22, 23), (24, 25)
NEW = (26, 27)
SLOTS = 28
DIAG, DDIAG, SQUARE, DSQUARE = 0, 1, 2, 3


def kernel(n, ham_hbm, pert_hbm, dens_ref, resp_ref, ham_ref, pert_ref, split, state, near,
           raw, partial, outbox, inbox, stat_out, stat_in, load_sem, send_sem, recv_sem,
           stat_send, stat_recv, ring_sem, late_sem):
    b = ham_hbm.shape[-1]
    h = b // 2
    groups = n // GROUP
    me = lax.axis_index("chain")
    group, local = me // GROUP, lax.rem(me, GROUP)
    inner = jnp.logical_and(local != 0, local != GROUP - 1)
    ring_low = jnp.logical_or(me == 0, jnp.logical_and(local == GROUP - 1, me != n - 1))
    ring_high = jnp.logical_or(me == n - 1, jnp.logical_and(local == 0, me != 0))
    soon = 2 * me < n
    odd = lax.rem(me, 2)
    sides = (me + 1 - 2 * odd, lax.rem(me - 1 + 2 * odd + n, n))
    place = (2 - 2 * odd, 2 * odd)

    def load(which, k):
        src, dst = ((ham_hbm, ham_ref), (pert_hbm, pert_ref))[which]
        return pltpu.make_async_copy(src.at[0, k], dst.at[0, k], load_sem.at[which, k])

    for which, k in ((0, 1), (1, 1), (0, 0), (0, 2), (1, 0), (1, 2)):
        load(which, k).start()

    def signal(sem, other):
        pl.semaphore_signal(sem, inc=1, device_id=(other,), device_id_type=MESH)

    barrier = pltpu.get_barrier_semaphore()
    for off in range(1, GROUP):
        signal(barrier, group * GROUP + lax.rem(local + off, GROUP))

    @pl.loop(group + 1, groups)
    def _(other):
        signal(barrier, other * GROUP + local)

    @pl.when(ring_low)
    def _():
        signal(barrier, sides[1])

    row_h = lax.broadcasted_iota(jnp.int32, (h, h), 0)
    col_h = lax.broadcasted_iota(jnp.int32, (h, h), 1)
    row_b = lax.broadcasted_iota(jnp.int32, (b, b), 0)
    col_b = lax.broadcasted_iota(jnp.int32, (b, b), 1)
    eye = row_b == col_b

    def pack(step, kind, m):
        corner = m[h:, h:]
        outbox[step, kind, 0:h] = m[:h, h:]
        outbox[step, kind, h : 2 * h] = jnp.where(row_h <= col_h, m[:h, :h], corner)
        diag = jnp.sum(jnp.where(row_h == col_h, corner, 0.0), axis=0, keepdims=True)
        outbox[step, kind, 2 * h : 2 * h + 8] = jnp.broadcast_to(diag, (8, h))

    def unpack(step, kind, q):
        off = inbox[step, kind, q, 0:h]
        mixed = inbox[step, kind, q, h : 2 * h]
        diag = inbox[step, kind, q, 2 * h : 2 * h + 1]
        turned = mixed.T
        first = jnp.where(row_h <= col_h, mixed, turned)
        last = jnp.where(row_h > col_h, mixed, jnp.where(row_h == col_h, diag, turned))
        return jnp.concatenate(
            [jnp.concatenate([first, off], axis=1), jnp.concatenate([off.T, last], axis=1)],
            axis=0,
        )

    def copy(step, kind, q):
        return pltpu.make_async_remote_copy(
            src_ref=outbox.at[step, kind, pl.ds(0, 2 * h + 2)],
            dst_ref=inbox.at[step, kind, q, pl.ds(0, 2 * h + 2)],
            send_sem=send_sem.at[step, kind, q],
            recv_sem=recv_sem.at[step, kind, q],
            device_id=(sides[q],),
            device_id_type=MESH,
        )

    def send(step, kind):
        for q in (1, 0):
            copy(step, kind, q).start()

    def arrived(step, kind, q):
        copy(step, kind, q).wait_recv()

    def put(slot, m):
        high = m.astype(BF16)
        split[slot, 0] = high
        split[slot, 1] = (m - high.astype(F32)).astype(BF16)

    def product(a, c, turned):
        dims = (((1,), (1 if turned else 0,)), ((), ()))
        out = None
        for u, v in ((0, 0), (0, 1), (1, 0)):
            part = lax.dot_general(split[a, u], split[c, v], dims, preferred_element_type=F32)
            out = part if out is None else out + part
        return out

    def total(*terms, turned=()):
        out = None
        for flag, group in ((False, terms), (True, turned)):
            for a, c in group:
                part = product(a, c, flag)
                out = part if out is None else out + part
        return out

    def sym(m):
        return 0.5 * (m + m.T)

    lane = lax.broadcasted_iota(jnp.int32, (1, 128), 1)

    def stat_copy(stage, mine, other):
        return pltpu.make_async_remote_copy(
            src_ref=stat_out.at[stage],
            dst_ref=stat_in.at[stage, mine],
            send_sem=stat_send.at[stage],
            recv_sem=stat_recv.at[stage],
            device_id=(other,),
            device_id_type=MESH,
        )

    def stat_all(stage, count):
        rows = stat_in.at[stage, pl.ds(0, count)]
        return pltpu.make_async_remote_copy(
            src_ref=rows,
            dst_ref=rows,
            send_sem=stat_send.at[stage],
            recv_sem=stat_recv.at[stage],
            device_id=(sides[0],),
            device_id_type=MESH,
        )

    def merged(stage, count):
        stats = stat_in[stage, 0:count].reshape(count, 128)
        return jnp.where(
            lane == 0,
            jnp.sum(stats, axis=0, keepdims=True),
            jnp.max(stats, axis=0, keepdims=True),
        )

    load(0, 1).wait()
    centre = ham_ref[0, 1]
    pack(0, DIAG, centre)
    load(0, 0).wait()
    load(0, 2).wait()
    onsite = jnp.sum(jnp.where(eye, centre, 0.0), axis=1, keepdims=True)
    reach = jnp.sum(
        jnp.abs(ham_ref[0, 0]) + jnp.abs(centre) + jnp.abs(ham_ref[0, 2]), axis=1, keepdims=True
    ) - jnp.abs(onsite)
    level = jnp.sum(onsite, axis=0, keepdims=True)
    mine = jnp.where(
        lane == 0,
        level,
        jnp.where(
            lane == 1,
            jnp.max(onsite + reach, axis=0, keepdims=True),
            jnp.max(reach - onsite, axis=0, keepdims=True),
        ),
    )
    stat_out[0] = mine
    stat_in[0, local] = mine
    level = level / b
    load(1, 1).wait()
    pack(0, DDIAG, pert_ref[0, 1])
    pl.semaphore_wait(barrier, GROUP - 1 + group + ring_high.astype(jnp.int32))

    @pl.loop(0, group)
    def _(other):
        signal(late_sem, other * GROUP + local)

    @pl.when(ring_high)
    def _():
        signal(ring_sem, sides[1])

    for off in range(1, GROUP):
        stat_copy(0, local, group * GROUP + lax.rem(local + off, GROUP)).start()

    @pl.when(inner)
    def _():
        copy(0, DIAG, 1).start()

    copy(0, DIAG, 0).start()

    @pl.when(jnp.logical_and(inner, soon))
    def _():
        send(0, DDIAG)

    put(D, 2.0 * (centre - jnp.where(eye, level, 0.0)))
    for q in (0, 1):
        put(E[q], ham_ref[0, place[q]])
    twice = total((D, D))
    wings = total(turned=((E[0], E[0]), (E[1], E[1])))
    square = 0.5 * twice + wings
    pack(0, SQUARE, square)
    outbox[0, SQUARE, 2 * h + 1 : 2 * h + 2] = jnp.broadcast_to(level, (1, h))
    raw[0] = square
    raw[1] = 0.125 * twice + wings

    stat_all(0, GROUP - 1).wait_recv()
    mine = merged(0, GROUP)
    stat_out[1] = mine
    stat_in[1, group] = mine

    @pl.when(group < groups - 1)
    def _():
        pl.semaphore_wait(late_sem, groups - 1 - group)

    @pl.loop(1, groups)
    def _(off):
        stat_copy(1, group, lax.rem(group + off, groups) * GROUP + local).start()

    @pl.when(ring_low)
    def _():
        pl.semaphore_wait(ring_sem, 1)

    @pl.when(jnp.logical_not(inner))
    def _():
        copy(0, DIAG, 1).start()

    @pl.when(jnp.logical_not(jnp.logical_and(inner, soon)))
    def _():
        send(0, DDIAG)

    send(0, SQUARE)
    load(1, 0).wait()
    load(1, 2).wait()
    put(DD, 2.0 * pert_ref[0, 1])
    for q in (0, 1):
        put(DE[q], pert_ref[0, place[q]])
    twice = total((D, DD))
    wings = total(turned=((E[0], DE[0]), (E[1], DE[1])))
    square = 0.5 * twice + wings
    square = square + square.T
    pack(0, DSQUARE, square)
    send(0, DSQUARE)
    raw[2] = square
    square = 0.125 * twice + wings
    raw[3] = square + square.T
    stat_all(1, groups - 1).wait_recv()
    stats = merged(1, groups)
    energy = stats[:, 0:1] / (n * b)
    bound = jnp.maximum(stats[:, 1:2] - energy, energy + stats[:, 2:3]) + 1e-6
    inverse = 1.0 / bound
    second = inverse * inverse

    g = (energy - level) * inverse
    node = (jnp.where(eye, energy, 0.0) - ham_ref[0, 1]) * inverse
    dnode = -pert_ref[0, 1] * inverse
    state[0, 0] = node
    state[1, 0] = dnode
    put(D, 2.0 * node)
    put(DD, 2.0 * dnode)
    for q in (0, 1):
        edge, dedge = -ham_ref[0, place[q]] * inverse, -pert_ref[0, place[q]] * inverse
        state[0, 1 + q] = edge
        state[1, 1 + q] = dedge
        put(E[q], edge)
        put(DE[q], dedge)
    put(A, raw[0] * second + (4.0 * g) * node - jnp.where(eye, 2.0 * g * g, 0.0))
    put(T, raw[1] * second + g * node - jnp.where(eye, 0.5 * g * g, 0.0))
    put(DA, raw[2] * second + (4.0 * g) * dnode)
    put(DT, raw[3] * second + g * dnode)

    def iterate(step, first, last):
        def pick(yes, no):
            return no if first is False else jnp.where(first, yes, no)

        def shift(q):
            return (energy - inbox[0, SQUARE, q, 2 * h + 1 : 2 * h + 2, 0:1]) * inverse

        for q in (0, 1):
            arrived(step, DIAG, q)
            other = unpack(step, DIAG, q)
            if first is not False:
                other = other * pick(-inverse, 1.0) + jnp.where(eye, pick(energy * inverse, 0.0), 0.0)
            near[0, q] = other
            put(DN[q], other)
            put(F[q], total((E[q], DN[q])))
        node = 1.5 * state[0, 0] - 0.5 * sym(
            total((D, T), turned=((F[0], E[0]), (F[1], E[1])))
        )
        if last:
            dens_ref[0, 1] = jnp.where(eye, 0.5, 0.0) - 0.5 * node
        else:
            state[0, 0] = node
            pack(step + 1, DIAG, node)
            send(step + 1, DIAG)
        for q in (0, 1):
            partial[0, q] = total((A, E[q]), (D, F[q]))

        for q in (0, 1):
            v = total((DE[q], DN[q]))
            arrived(step, DDIAG, q)
            other = unpack(step, DDIAG, q)
            if first is not False:
                other = other * pick(-inverse, 1.0)
            near[1, q] = other
            put(DDN[q], other)
            u = total((E[q], DDN[q]))
            put(U[q], u + v)
            put(V[q], u + 2.0 * v)
        dnode = 1.5 * state[1, 0] - 0.5 * sym(
            total((DD, T), (D, DT), turned=((V[0], E[0]), (V[1], E[1])))
        )
        if last:
            resp_ref[0, 1] = (-0.5 * bound) * dnode
        else:
            state[1, 0] = dnode
            pack(step + 1, DDIAG, dnode)
            send(step + 1, DDIAG)
        for q in (0, 1):
            partial[1, q] = total((DA, E[q]), (A, DE[q]), (DD, F[q]), (D, U[q]))

        for q in (0, 1):
            arrived(step, SQUARE, q)
            other = unpack(step, SQUARE, q)
            if first is not False:
                g = shift(q)
                other = (
                    other * pick(second, 1.0)
                    + pick(4.0 * g, 0.0) * near[0, q]
                    - jnp.where(eye, pick(2.0 * g * g, 0.0), 0.0)
                )
            put(AN[q], other)
            edge = 1.5 * state[0, 1 + q] - 0.25 * (partial[0, q] + total((E[q], AN[q])))
            if last:
                dens_ref[0, place[q]] = -0.5 * edge
            else:
                state[0, 1 + q] = edge
                put(NEW[q], edge)
        if not last:
            put(D, 2.0 * state[0, 0])
            twice = total((D, D))
            wings = total(turned=((NEW[0], NEW[0]), (NEW[1], NEW[1])))
            square = 0.5 * twice + wings
            pack(step + 1, SQUARE, square)
            send(step + 1, SQUARE)
            put(A, square)
            put(T, 0.125 * twice + wings)
        for q in (0, 1):
            partial[1, q] += total((DE[q], AN[q]))

        for q in (0, 1):
            arrived(step, DSQUARE, q)
            other = unpack(step, DSQUARE, q)
            if first is not False:
                other = other * pick(second, 1.0) + pick(4.0 * shift(q), 0.0) * near[1, q]
            put(DAN[q], other)
            dedge = 1.5 * state[1, 1 + q] - 0.25 * (partial[1, q] + total((E[q], DAN[q])))
            if last:
                resp_ref[0, place[q]] = (-0.5 * bound) * dedge
            else:
                state[1, 1 + q] = dedge
                put(DE[q], dedge)
        if not last:
            put(DD, 2.0 * state[1, 0])
            for q in (0, 1):
                split[E[q]] = split[NEW[q]]
            twice = total((D, DD))
            wings = total(turned=((E[0], DE[0]), (E[1], DE[1])))
            square = 0.5 * twice + wings
            square = square + square.T
            pack(step + 1, DSQUARE, square)
            send(step + 1, DSQUARE)
            put(DA, square)
            square = 0.125 * twice + wings
            put(DT, square + square.T)

    @pl.loop(0, ITERS - 1)
    def _(step):
        iterate(step, step == 0, False)

    iterate(ITERS - 1, False, True)

    stat_all(0, GROUP - 1).wait_send()
    stat_all(1, groups - 1).wait_send()
    for step in range(ITERS):
        for kind in range(4):
            for q in (0, 1):
                copy(step, kind, q).wait_send()


def per_device(n, ham, pert):
    b = ham.shape[-1]
    packed = (b + 8, b // 2)
    count = max(GROUP, n // GROUP)
    return pl.pallas_call(
        functools.partial(kernel, n),
        out_shape=(jax.ShapeDtypeStruct(ham.shape, F32), jax.ShapeDtypeStruct(ham.shape, F32)),
        in_specs=[pl.BlockSpec(memory_space=pltpu.HBM)] * 2,
        out_specs=[pl.BlockSpec(memory_space=pltpu.VMEM)] * 2,
        scratch_shapes=[
            pltpu.VMEM(ham.shape, F32),
            pltpu.VMEM(pert.shape, F32),
            pltpu.VMEM((SLOTS, 2, b, b), BF16),
            pltpu.VMEM((2, 3, b, b), F32),
            pltpu.VMEM((2, 2, b, b), F32),
            pltpu.VMEM((4, b, b), F32),
            pltpu.VMEM((2, 2, b, b), F32),
            pltpu.VMEM((ITERS, 4) + packed, F32),
            pltpu.VMEM((ITERS, 4, 2) + packed, F32),
            pltpu.VMEM((2, 1, 128), F32),
            pltpu.VMEM((2, count, 1, 128), F32),
            pltpu.SemaphoreType.DMA((2, 3)),
            pltpu.SemaphoreType.DMA((ITERS, 4, 2)),
            pltpu.SemaphoreType.DMA((ITERS, 4, 2)),
            pltpu.SemaphoreType.DMA((2,)),
            pltpu.SemaphoreType.DMA((2,)),
            pltpu.SemaphoreType.REGULAR,
            pltpu.SemaphoreType.REGULAR,
        ],
        compiler_params=pltpu.CompilerParams(
            collective_id=0, has_side_effects=True, vmem_limit_bytes=52 * 1024 * 1024
        ),
    )(ham, pert)


def solution(mesh):
    n = mesh.shape["chain"]
    spec = P("chain", None, None, None)
    return jax.shard_map(
        functools.partial(per_device, n),
        mesh=mesh,
        in_specs=(spec, spec),
        out_specs=(spec, spec),
        check_vma=False,
    )
```

```python
import functools

import jax
import jax.numpy as jnp
from jax import lax
from jax.experimental import pallas as pl
from jax.experimental.pallas import tpu as pltpu
from jax.sharding import PartitionSpec as P

ITERS = 3
AHEAD = 2
GROUP = 8
F32, BF16 = jnp.float32, jnp.bfloat16
MESH = pl.DeviceIdType.MESH

D, DD = 0, 1
E, DE = (2, 3), (4, 5)
DN, DDN = (6, 7), (8, 9)
AN, DAN = (10, 11), (12, 13)
A, DA, T, DT = 14, 15, 16, 17
F, U, V, W = (18, 19), (20, 21), (22, 23), (24, 25)
NEW = (26, 27)
SLOTS = 28
DIAG, DDIAG, SQUARE, DSQUARE = 0, 1, 2, 3


def kernel(n, ham_hbm, pert_hbm, dens_ref, resp_ref, ham_ref, pert_ref, split, state, near,
           raw, partial, outbox, inbox, stat_out, stat_in, load_sem, send_sem, recv_sem,
           stat_send, stat_recv, ring_sem, late_sem):
    b = ham_hbm.shape[-1]
    h = b // 2
    groups = n // GROUP
    me = lax.axis_index("chain")
    group, local = me // GROUP, lax.rem(me, GROUP)
    inner = jnp.logical_and(local != 0, local != GROUP - 1)
    ring_low = jnp.logical_or(me == 0, jnp.logical_and(local == GROUP - 1, me != n - 1))
    ring_high = jnp.logical_or(me == n - 1, jnp.logical_and(local == 0, me != 0))
    soon = 2 * me < n
    odd = lax.rem(me, 2)
    sides = (me + 1 - 2 * odd, lax.rem(me - 1 + 2 * odd + n, n))
    place = (2 - 2 * odd, 2 * odd)

    def load(which, k):
        src, dst = ((ham_hbm, ham_ref), (pert_hbm, pert_ref))[which]
        return pltpu.make_async_copy(src.at[0, k], dst.at[0, k], load_sem.at[which, k])

    for which, k in ((0, 1), (1, 1), (0, 0), (0, 2), (1, 0), (1, 2)):
        load(which, k).start()

    def signal(sem, other):
        pl.semaphore_signal(sem, inc=1, device_id=(other,), device_id_type=MESH)

    barrier = pltpu.get_barrier_semaphore()
    for off in range(1, GROUP):
        signal(barrier, group * GROUP + lax.rem(local + off, GROUP))

    @pl.loop(group + 1, groups)
    def _(other):
        signal(barrier, other * GROUP + local)

    @pl.when(ring_low)
    def _():
        signal(barrier, sides[1])

    row_h = lax.broadcasted_iota(jnp.int32, (h, h), 0)
    col_h = lax.broadcasted_iota(jnp.int32, (h, h), 1)
    row_b = lax.broadcasted_iota(jnp.int32, (b, b), 0)
    col_b = lax.broadcasted_iota(jnp.int32, (b, b), 1)
    eye = row_b == col_b

    def pack(step, kind, m):
        corner = m[h:, h:]
        outbox[step, kind, 0:h] = m[:h, h:]
        outbox[step, kind, h : 2 * h] = jnp.where(row_h <= col_h, m[:h, :h], corner)
        diag = jnp.sum(jnp.where(row_h == col_h, corner, 0.0), axis=0, keepdims=True)
        outbox[step, kind, 2 * h : 2 * h + 8] = jnp.broadcast_to(diag, (8, h))

    def unpack(step, kind, q):
        off = inbox[step, kind, q, 0:h]
        mixed = inbox[step, kind, q, h : 2 * h]
        diag = inbox[step, kind, q, 2 * h : 2 * h + 1]
        turned = mixed.T
        first = jnp.where(row_h <= col_h, mixed, turned)
        last = jnp.where(row_h > col_h, mixed, jnp.where(row_h == col_h, diag, turned))
        return jnp.concatenate(
            [jnp.concatenate([first, off], axis=1), jnp.concatenate([off.T, last], axis=1)],
            axis=0,
        )

    def copy(step, kind, q):
        return pltpu.make_async_remote_copy(
            src_ref=outbox.at[step, kind, pl.ds(0, 2 * h + 2)],
            dst_ref=inbox.at[step, kind, q, pl.ds(0, 2 * h + 2)],
            send_sem=send_sem.at[step, kind, q],
            recv_sem=recv_sem.at[step, kind, q],
            device_id=(sides[q],),
            device_id_type=MESH,
        )

    def send(step, kind):
        for q in (1, 0):
            copy(step, kind, q).start()

    def send_late(step, kind):
        @pl.when(inner)
        def _():
            copy(step, kind, 1).start()

        copy(step, kind, 0).start()

    def follow(step, kind):
        step, kind = step + (kind + AHEAD) // 4, (kind + AHEAD) % 4
        valid = jnp.logical_and(step > 0, step < ITERS)

        @pl.when(jnp.logical_and(jnp.logical_not(inner), valid))
        def _():
            copy(jnp.minimum(step, ITERS - 1), kind, 1).start()

    def arrived(step, kind, q):
        copy(step, kind, q).wait_recv()
        if q == 0:
            follow(step, kind)

    def put(slot, m):
        high = m.astype(BF16)
        split[slot, 0] = high
        split[slot, 1] = (m - high.astype(F32)).astype(BF16)

    def product(a, c, turned):
        dims = (((1,), (1 if turned else 0,)), ((), ()))
        out = None
        for u, v in ((0, 0), (0, 1), (1, 0)):
            part = lax.dot_general(split[a, u], split[c, v], dims, preferred_element_type=F32)
            out = part if out is None else out + part
        return out

    def total(*terms, turned=()):
        out = None
        for flag, group in ((False, terms), (True, turned)):
            for a, c in group:
                part = product(a, c, flag)
                out = part if out is None else out + part
        return out

    def sym(m):
        return 0.5 * (m + m.T)

    lane = lax.broadcasted_iota(jnp.int32, (1, 128), 1)

    def stat_copy(stage, mine, other):
        return pltpu.make_async_remote_copy(
            src_ref=stat_out.at[stage],
            dst_ref=stat_in.at[stage, mine],
            send_sem=stat_send.at[stage],
            recv_sem=stat_recv.at[stage],
            device_id=(other,),
            device_id_type=MESH,
        )

    def stat_all(stage, count):
        rows = stat_in.at[stage, pl.ds(0, count)]
        return pltpu.make_async_remote_copy(
            src_ref=rows,
            dst_ref=rows,
            send_sem=stat_send.at[stage],
            recv_sem=stat_recv.at[stage],
            device_id=(sides[0],),
            device_id_type=MESH,
        )

    def merged(stage, count):
        stats = stat_in[stage, 0:count].reshape(count, 128)
        return jnp.where(
            lane == 0,
            jnp.sum(stats, axis=0, keepdims=True),
            jnp.max(stats, axis=0, keepdims=True),
        )

    load(0, 1).wait()
    centre = ham_ref[0, 1]
    pack(0, DIAG, centre)
    load(0, 0).wait()
    load(0, 2).wait()
    onsite = jnp.sum(jnp.where(eye, centre, 0.0), axis=1, keepdims=True)
    reach = jnp.sum(
        jnp.abs(ham_ref[0, 0]) + jnp.abs(centre) + jnp.abs(ham_ref[0, 2]), axis=1, keepdims=True
    ) - jnp.abs(onsite)
    level = jnp.sum(onsite, axis=0, keepdims=True)
    mine = jnp.where(
        lane == 0,
        level,
        jnp.where(
            lane == 1,
            jnp.max(onsite + reach, axis=0, keepdims=True),
            jnp.max(reach - onsite, axis=0, keepdims=True),
        ),
    )
    stat_out[0] = mine
    stat_in[0, local] = mine
    level = level / b
    load(1, 1).wait()
    pack(0, DDIAG, pert_ref[0, 1])
    pl.semaphore_wait(barrier, GROUP - 1 + group + ring_high.astype(jnp.int32))

    @pl.loop(0, group)
    def _(other):
        signal(late_sem, other * GROUP + local)

    @pl.when(ring_high)
    def _():
        signal(ring_sem, sides[1])

    for off in range(1, GROUP):
        stat_copy(0, local, group * GROUP + lax.rem(local + off, GROUP)).start()

    @pl.when(inner)
    def _():
        copy(0, DIAG, 1).start()

    copy(0, DIAG, 0).start()

    @pl.when(jnp.logical_and(inner, soon))
    def _():
        send(0, DDIAG)

    put(D, 2.0 * (centre - jnp.where(eye, level, 0.0)))
    for q in (0, 1):
        put(E[q], ham_ref[0, place[q]])
    twice = total((D, D))
    wings = total(turned=((E[0], E[0]), (E[1], E[1])))
    square = 0.5 * twice + wings
    pack(0, SQUARE, square)
    outbox[0, SQUARE, 2 * h + 1 : 2 * h + 2] = jnp.broadcast_to(level, (1, h))
    raw[0] = square
    raw[1] = 0.125 * twice + wings

    stat_all(0, GROUP - 1).wait_recv()
    mine = merged(0, GROUP)
    stat_out[1] = mine
    stat_in[1, group] = mine

    @pl.when(group < groups - 1)
    def _():
        pl.semaphore_wait(late_sem, groups - 1 - group)

    @pl.loop(1, groups)
    def _(off):
        stat_copy(1, group, lax.rem(group + off, groups) * GROUP + local).start()

    @pl.when(ring_low)
    def _():
        pl.semaphore_wait(ring_sem, 1)

    @pl.when(jnp.logical_not(inner))
    def _():
        copy(0, DIAG, 1).start()

    @pl.when(jnp.logical_not(jnp.logical_and(inner, soon)))
    def _():
        send(0, DDIAG)

    send(0, SQUARE)
    load(1, 0).wait()
    load(1, 2).wait()
    put(DD, 2.0 * pert_ref[0, 1])
    for q in (0, 1):
        put(DE[q], pert_ref[0, place[q]])
    twice = total((D, DD))
    wings = total(turned=((E[0], DE[0]), (E[1], DE[1])))
    square = 0.5 * twice + wings
    square = square + square.T
    pack(0, DSQUARE, square)
    send(0, DSQUARE)
    raw[2] = square
    square = 0.125 * twice + wings
    raw[3] = square + square.T
    stat_all(1, groups - 1).wait_recv()
    stats = merged(1, groups)
    energy = stats[:, 0:1] / (n * b)
    bound = jnp.maximum(stats[:, 1:2] - energy, energy + stats[:, 2:3]) + 1e-6
    inverse = 1.0 / bound
    second = inverse * inverse

    g = (energy - level) * inverse
    node = (jnp.where(eye, energy, 0.0) - ham_ref[0, 1]) * inverse
    dnode = -pert_ref[0, 1] * inverse
    state[0, 0] = node
    state[1, 0] = dnode
    put(D, 2.0 * node)
    put(DD, 2.0 * dnode)
    for q in (0, 1):
        edge, dedge = -ham_ref[0, place[q]] * inverse, -pert_ref[0, place[q]] * inverse
        state[0, 1 + q] = edge
        state[1, 1 + q] = dedge
        put(E[q], edge)
        put(DE[q], dedge)
    put(A, raw[0] * second + (4.0 * g) * node - jnp.where(eye, 2.0 * g * g, 0.0))
    put(T, raw[1] * second + g * node - jnp.where(eye, 0.5 * g * g, 0.0))
    put(DA, raw[2] * second + (4.0 * g) * dnode)
    put(DT, raw[3] * second + g * dnode)

    def iterate(step, first, last):
        def pick(yes, no):
            return no if first is False else jnp.where(first, yes, no)

        def shift(q):
            return (energy - inbox[0, SQUARE, q, 2 * h + 1 : 2 * h + 2, 0:1]) * inverse

        for q in (0, 1):
            arrived(step, DIAG, q)
            other = unpack(step, DIAG, q)
            if first is not False:
                other = other * pick(-inverse, 1.0) + jnp.where(eye, pick(energy * inverse, 0.0), 0.0)
            near[0, q] = other
            put(DN[q], other)
            put(F[q], total((E[q], DN[q])))
        node = 1.5 * state[0, 0] - 0.5 * sym(
            total((D, T), turned=((F[0], E[0]), (F[1], E[1])))
        )
        if last:
            dens_ref[0, 1] = jnp.where(eye, 0.5, 0.0) - 0.5 * node
        else:
            state[0, 0] = node
            pack(step + 1, DIAG, node)
            send_late(step + 1, DIAG)
        for q in (0, 1):
            partial[0, q] = total((A, E[q]), (D, F[q]))

        for q in (0, 1):
            v = total((DE[q], DN[q]))
            arrived(step, DDIAG, q)
            other = unpack(step, DDIAG, q)
            if first is not False:
                other = other * pick(-inverse, 1.0)
            near[1, q] = other
            put(DDN[q], other)
            u = total((E[q], DDN[q]))
            put(U[q], u + v)
            put(V[q], u + 2.0 * v)
        dnode = 1.5 * state[1, 0] - 0.5 * sym(
            total((DD, T), (D, DT), turned=((V[0], E[0]), (V[1], E[1])))
        )
        if last:
            resp_ref[0, 1] = (-0.5 * bound) * dnode
        else:
            state[1, 0] = dnode
            pack(step + 1, DDIAG, dnode)
            send_late(step + 1, DDIAG)
        for q in (0, 1):
            partial[1, q] = total((DA, E[q]), (A, DE[q]), (DD, F[q]), (D, U[q]))

        for q in (0, 1):
            arrived(step, SQUARE, q)
            other = unpack(step, SQUARE, q)
            if first is not False:
                g = shift(q)
                other = (
                    other * pick(second, 1.0)
                    + pick(4.0 * g, 0.0) * near[0, q]
                    - jnp.where(eye, pick(2.0 * g * g, 0.0), 0.0)
                )
            put(AN[q], other)
            edge = 1.5 * state[0, 1 + q] - 0.25 * (partial[0, q] + total((E[q], AN[q])))
            if last:
                dens_ref[0, place[q]] = -0.5 * edge
            else:
                state[0, 1 + q] = edge
                put(NEW[q], edge)
        if not last:
            put(D, 2.0 * state[0, 0])
            twice = total((D, D))
            wings = total(turned=((NEW[0], NEW[0]), (NEW[1], NEW[1])))
            square = 0.5 * twice + wings
            pack(step + 1, SQUARE, square)
            send_late(step + 1, SQUARE)
            put(A, square)
            put(T, 0.125 * twice + wings)
        for q in (0, 1):
            partial[1, q] += total((DE[q], AN[q]))

        for q in (0, 1):
            arrived(step, DSQUARE, q)
            other = unpack(step, DSQUARE, q)
            if first is not False:
                other = other * pick(second, 1.0) + pick(4.0 * shift(q), 0.0) * near[1, q]
            put(DAN[q], other)
            dedge = 1.5 * state[1, 1 + q] - 0.25 * (partial[1, q] + total((E[q], DAN[q])))
            if last:
                resp_ref[0, place[q]] = (-0.5 * bound) * dedge
            else:
                state[1, 1 + q] = dedge
                put(DE[q], dedge)
        if not last:
            put(DD, 2.0 * state[1, 0])
            for q in (0, 1):
                split[E[q]] = split[NEW[q]]
            twice = total((D, DD))
            wings = total(turned=((E[0], DE[0]), (E[1], DE[1])))
            square = 0.5 * twice + wings
            square = square + square.T
            pack(step + 1, DSQUARE, square)
            send_late(step + 1, DSQUARE)
            put(DA, square)
            square = 0.125 * twice + wings
            put(DT, square + square.T)

    @pl.loop(0, ITERS - 1)
    def _(step):
        iterate(step, step == 0, False)

    iterate(ITERS - 1, False, True)

    stat_all(0, GROUP - 1).wait_send()
    stat_all(1, groups - 1).wait_send()
    for step in range(ITERS):
        for kind in range(4):
            for q in (0, 1):
                copy(step, kind, q).wait_send()


def store(dens_ref, resp_ref, dens_hbm, resp_hbm, sem):
    moves = [
        pltpu.make_async_copy(src.at[0, k], dst.at[0, k], sem.at[which, k])
        for which, (src, dst) in enumerate(((dens_ref, dens_hbm), (resp_ref, resp_hbm)))
        for k in range(3)
    ]
    for move in moves:
        move.start()
    for move in moves:
        move.wait()


def per_device(n, ham, pert):
    b = ham.shape[-1]
    packed = (b + 8, b // 2)
    count = max(GROUP, n // GROUP)
    out = pl.pallas_call(
        functools.partial(kernel, n),
        out_shape=(jax.ShapeDtypeStruct(ham.shape, F32), jax.ShapeDtypeStruct(ham.shape, F32)),
        in_specs=[pl.BlockSpec(memory_space=pltpu.HBM)] * 2,
        out_specs=[pl.BlockSpec(memory_space=pltpu.VMEM)] * 2,
        scratch_shapes=[
            pltpu.VMEM(ham.shape, F32),
            pltpu.VMEM(pert.shape, F32),
            pltpu.VMEM((SLOTS, 2, b, b), BF16),
            pltpu.VMEM((2, 3, b, b), F32),
            pltpu.VMEM((2, 2, b, b), F32),
            pltpu.VMEM((4, b, b), F32),
            pltpu.VMEM((2, 2, b, b), F32),
            pltpu.VMEM((ITERS, 4) + packed, F32),
            pltpu.VMEM((ITERS, 4, 2) + packed, F32),
            pltpu.VMEM((2, 1, 128), F32),
            pltpu.VMEM((2, count, 1, 128), F32),
            pltpu.SemaphoreType.DMA((2, 3)),
            pltpu.SemaphoreType.DMA((ITERS, 4, 2)),
            pltpu.SemaphoreType.DMA((ITERS, 4, 2)),
            pltpu.SemaphoreType.DMA((2,)),
            pltpu.SemaphoreType.DMA((2,)),
            pltpu.SemaphoreType.REGULAR,
            pltpu.SemaphoreType.REGULAR,
        ],
        compiler_params=pltpu.CompilerParams(
            collective_id=0, has_side_effects=True, vmem_limit_bytes=52 * 1024 * 1024
        ),
    )(ham, pert)
    return pl.pallas_call(
        store,
        out_shape=(jax.ShapeDtypeStruct(ham.shape, F32), jax.ShapeDtypeStruct(ham.shape, F32)),
        in_specs=[pl.BlockSpec(memory_space=pl.ANY)] * 2,
        out_specs=[pl.BlockSpec(memory_space=pltpu.HBM)] * 2,
        scratch_shapes=[pltpu.SemaphoreType.DMA((2, 3))],
        compiler_params=pltpu.CompilerParams(vmem_limit_bytes=1024 * 1024),
    )(*out)


def solution(mesh):
    n = mesh.shape["chain"]
    spec = P("chain", None, None, None)
    return jax.shard_map(
        functools.partial(per_device, n),
        mesh=mesh,
        in_specs=(spec, spec),
        out_specs=(spec, spec),
        check_vma=False,
    )
```

```python
import functools

import jax
import jax.numpy as jnp
from jax import lax
from jax.experimental import pallas as pl
from jax.experimental.pallas import tpu as pltpu
from jax.sharding import PartitionSpec as P

ITERS = 3
AHEAD = ((2,), (), (1, 2), (2,))
AHEAD_ENDS = ((2,), (2,), (2,), (2,))
GROUP = 8
F32, BF16 = jnp.float32, jnp.bfloat16
MESH = pl.DeviceIdType.MESH

D, DD = 0, 1
E, DE = (2, 3), (4, 5)
DN, DDN = (6, 7), (8, 9)
AN, DAN = (10, 11), (12, 13)
A, DA, T, DT = 14, 15, 16, 17
F, U, V, W = (18, 19), (20, 21), (22, 23), (24, 25)
NEW = (26, 27)
SLOTS = 28
DIAG, DDIAG, SQUARE, DSQUARE = 0, 1, 2, 3


def kernel(n, ham_hbm, pert_hbm, dens_ref, resp_ref, ham_ref, pert_ref, split, state, near,
           raw, partial, outbox, inbox, stat_out, stat_in, load_sem, send_sem, recv_sem,
           stat_send, stat_recv, ring_sem, late_sem):
    b = ham_hbm.shape[-1]
    h = b // 2
    groups = n // GROUP
    me = lax.axis_index("chain")
    group, local = me // GROUP, lax.rem(me, GROUP)
    inner = jnp.logical_and(local != 0, local != GROUP - 1)
    ring_low = jnp.logical_or(me == 0, jnp.logical_and(local == GROUP - 1, me != n - 1))
    ring_high = jnp.logical_or(me == n - 1, jnp.logical_and(local == 0, me != 0))
    soon = 2 * me < n
    ends = jnp.logical_or(me == 0, me == n - 1)
    middle = jnp.logical_not(jnp.logical_or(inner, ends))
    odd = lax.rem(me, 2)
    sides = (me + 1 - 2 * odd, lax.rem(me - 1 + 2 * odd + n, n))
    place = (2 - 2 * odd, 2 * odd)

    def load(which, k):
        src, dst = ((ham_hbm, ham_ref), (pert_hbm, pert_ref))[which]
        return pltpu.make_async_copy(src.at[0, k], dst.at[0, k], load_sem.at[which, k])

    for which, k in ((0, 1), (1, 1), (0, 0), (0, 2), (1, 0), (1, 2)):
        load(which, k).start()

    def signal(sem, other):
        pl.semaphore_signal(sem, inc=1, device_id=(other,), device_id_type=MESH)

    barrier = pltpu.get_barrier_semaphore()
    for off in range(1, GROUP):
        signal(barrier, group * GROUP + lax.rem(local + off, GROUP))

    @pl.loop(group + 1, groups)
    def _(other):
        signal(barrier, other * GROUP + local)

    @pl.when(ring_low)
    def _():
        signal(barrier, sides[1])

    row_h = lax.broadcasted_iota(jnp.int32, (h, h), 0)
    col_h = lax.broadcasted_iota(jnp.int32, (h, h), 1)
    row_b = lax.broadcasted_iota(jnp.int32, (b, b), 0)
    col_b = lax.broadcasted_iota(jnp.int32, (b, b), 1)
    eye = row_b == col_b

    def pack(step, kind, m):
        corner = m[h:, h:]
        outbox[step, kind, 0:h] = m[:h, h:]
        outbox[step, kind, h : 2 * h] = jnp.where(row_h <= col_h, m[:h, :h], corner)
        diag = jnp.sum(jnp.where(row_h == col_h, corner, 0.0), axis=0, keepdims=True)
        outbox[step, kind, 2 * h : 2 * h + 8] = jnp.broadcast_to(diag, (8, h))

    def unpack(step, kind, q):
        off = inbox[step, kind, q, 0:h]
        mixed = inbox[step, kind, q, h : 2 * h]
        diag = inbox[step, kind, q, 2 * h : 2 * h + 1]
        turned = mixed.T
        first = jnp.where(row_h <= col_h, mixed, turned)
        last = jnp.where(row_h > col_h, mixed, jnp.where(row_h == col_h, diag, turned))
        return jnp.concatenate(
            [jnp.concatenate([first, off], axis=1), jnp.concatenate([off.T, last], axis=1)],
            axis=0,
        )

    def copy(step, kind, q):
        return pltpu.make_async_remote_copy(
            src_ref=outbox.at[step, kind, pl.ds(0, 2 * h + 2)],
            dst_ref=inbox.at[step, kind, q, pl.ds(0, 2 * h + 2)],
            send_sem=send_sem.at[step, kind, q],
            recv_sem=recv_sem.at[step, kind, q],
            device_id=(sides[q],),
            device_id_type=MESH,
        )

    def send(step, kind):
        for q in (1, 0):
            copy(step, kind, q).start()

    def send_late(step, kind):
        @pl.when(inner)
        def _():
            copy(step, kind, 1).start()

        copy(step, kind, 0).start()

    def follow(step, kind, ahead, which):
        step, kind = step + (kind + ahead) // 4, (kind + ahead) % 4
        valid = jnp.logical_and(step > 0, step < ITERS)

        @pl.when(jnp.logical_and(which, valid))
        def _():
            copy(jnp.minimum(step, ITERS - 1), kind, 1).start()

    def arrived(step, kind, q):
        copy(step, kind, q).wait_recv()
        if q == 0:
            for ahead in AHEAD[kind]:
                follow(step, kind, ahead, middle)
            for ahead in AHEAD_ENDS[kind]:
                follow(step, kind, ahead, ends)

    def put(slot, m):
        high = m.astype(BF16)
        split[slot, 0] = high
        split[slot, 1] = (m - high.astype(F32)).astype(BF16)

    def product(a, c, turned):
        dims = (((1,), (1 if turned else 0,)), ((), ()))
        out = None
        for u, v in ((0, 0), (0, 1), (1, 0)):
            part = lax.dot_general(split[a, u], split[c, v], dims, preferred_element_type=F32)
            out = part if out is None else out + part
        return out

    def total(*terms, turned=()):
        out = None
        for flag, group in ((False, terms), (True, turned)):
            for a, c in group:
                part = product(a, c, flag)
                out = part if out is None else out + part
        return out

    def sym(m):
        return 0.5 * (m + m.T)

    lane = lax.broadcasted_iota(jnp.int32, (1, 128), 1)

    def stat_copy(stage, mine, other):
        return pltpu.make_async_remote_copy(
            src_ref=stat_out.at[stage],
            dst_ref=stat_in.at[stage, mine],
            send_sem=stat_send.at[stage],
            recv_sem=stat_recv.at[stage],
            device_id=(other,),
            device_id_type=MESH,
        )

    def stat_all(stage, count):
        rows = stat_in.at[stage, pl.ds(0, count)]
        return pltpu.make_async_remote_copy(
            src_ref=rows,
            dst_ref=rows,
            send_sem=stat_send.at[stage],
            recv_sem=stat_recv.at[stage],
            device_id=(sides[0],),
            device_id_type=MESH,
        )

    def merged(stage, count):
        stats = stat_in[stage, 0:count].reshape(count, 128)
        return jnp.where(
            lane == 0,
            jnp.sum(stats, axis=0, keepdims=True),
            jnp.max(stats, axis=0, keepdims=True),
        )

    load(0, 1).wait()
    centre = ham_ref[0, 1]
    pack(0, DIAG, centre)
    load(0, 0).wait()
    load(0, 2).wait()
    onsite = jnp.sum(jnp.where(eye, centre, 0.0), axis=1, keepdims=True)
    reach = jnp.sum(
        jnp.abs(ham_ref[0, 0]) + jnp.abs(centre) + jnp.abs(ham_ref[0, 2]), axis=1, keepdims=True
    ) - jnp.abs(onsite)
    level = jnp.sum(onsite, axis=0, keepdims=True)
    mine = jnp.where(
        lane == 0,
        level,
        jnp.where(
            lane == 1,
            jnp.max(onsite + reach, axis=0, keepdims=True),
            jnp.max(reach - onsite, axis=0, keepdims=True),
        ),
    )
    stat_out[0] = mine
    stat_in[0, local] = mine
    level = level / b
    load(1, 1).wait()
    pack(0, DDIAG, pert_ref[0, 1])
    pl.semaphore_wait(barrier, GROUP - 1 + group + ring_high.astype(jnp.int32))

    @pl.loop(0, group)
    def _(other):
        signal(late_sem, other * GROUP + local)

    @pl.when(ring_high)
    def _():
        signal(ring_sem, sides[1])

    for off in range(1, GROUP):
        stat_copy(0, local, group * GROUP + lax.rem(local + off, GROUP)).start()

    @pl.when(inner)
    def _():
        copy(0, DIAG, 1).start()

    copy(0, DIAG, 0).start()

    @pl.when(jnp.logical_and(inner, soon))
    def _():
        send(0, DDIAG)

    put(D, 2.0 * (centre - jnp.where(eye, level, 0.0)))
    for q in (0, 1):
        put(E[q], ham_ref[0, place[q]])
    twice = total((D, D))
    wings = total(turned=((E[0], E[0]), (E[1], E[1])))
    square = 0.5 * twice + wings
    pack(0, SQUARE, square)
    outbox[0, SQUARE, 2 * h + 1 : 2 * h + 2] = jnp.broadcast_to(level, (1, h))
    raw[0] = square
    raw[1] = 0.125 * twice + wings

    stat_all(0, GROUP - 1).wait_recv()
    mine = merged(0, GROUP)
    stat_out[1] = mine
    stat_in[1, group] = mine

    @pl.when(group < groups - 1)
    def _():
        pl.semaphore_wait(late_sem, groups - 1 - group)

    @pl.loop(1, groups)
    def _(off):
        stat_copy(1, group, lax.rem(group + off, groups) * GROUP + local).start()

    @pl.when(ring_low)
    def _():
        pl.semaphore_wait(ring_sem, 1)

    @pl.when(jnp.logical_not(inner))
    def _():
        copy(0, DIAG, 1).start()

    @pl.when(jnp.logical_not(jnp.logical_and(inner, soon)))
    def _():
        send(0, DDIAG)

    send(0, SQUARE)
    load(1, 0).wait()
    load(1, 2).wait()
    put(DD, 2.0 * pert_ref[0, 1])
    for q in (0, 1):
        put(DE[q], pert_ref[0, place[q]])
    twice = total((D, DD))
    wings = total(turned=((E[0], DE[0]), (E[1], DE[1])))
    square = 0.5 * twice + wings
    square = square + square.T
    pack(0, DSQUARE, square)
    send(0, DSQUARE)
    raw[2] = square
    square = 0.125 * twice + wings
    raw[3] = square + square.T
    stat_all(1, groups - 1).wait_recv()
    stats = merged(1, groups)
    energy = stats[:, 0:1] / (n * b)
    bound = jnp.maximum(stats[:, 1:2] - energy, energy + stats[:, 2:3]) + 1e-6
    inverse = 1.0 / bound
    second = inverse * inverse

    g = (energy - level) * inverse
    node = (jnp.where(eye, energy, 0.0) - ham_ref[0, 1]) * inverse
    dnode = -pert_ref[0, 1] * inverse
    state[0, 0] = node
    state[1, 0] = dnode
    put(D, 2.0 * node)
    put(DD, 2.0 * dnode)
    for q in (0, 1):
        edge, dedge = -ham_ref[0, place[q]] * inverse, -pert_ref[0, place[q]] * inverse
        state[0, 1 + q] = edge
        state[1, 1 + q] = dedge
        put(E[q], edge)
        put(DE[q], dedge)
    put(A, raw[0] * second + (4.0 * g) * node - jnp.where(eye, 2.0 * g * g, 0.0))
    put(T, raw[1] * second + g * node - jnp.where(eye, 0.5 * g * g, 0.0))
    put(DA, raw[2] * second + (4.0 * g) * dnode)
    put(DT, raw[3] * second + g * dnode)

    def iterate(step, first, last):
        def pick(yes, no):
            return no if first is False else jnp.where(first, yes, no)

        def shift(q):
            return (energy - inbox[0, SQUARE, q, 2 * h + 1 : 2 * h + 2, 0:1]) * inverse

        for q in (0, 1):
            arrived(step, DIAG, q)
            other = unpack(step, DIAG, q)
            if first is not False:
                other = other * pick(-inverse, 1.0) + jnp.where(eye, pick(energy * inverse, 0.0), 0.0)
            near[0, q] = other
            put(DN[q], other)
            put(F[q], total((E[q], DN[q])))
        node = 1.5 * state[0, 0] - 0.5 * sym(
            total((D, T), turned=((F[0], E[0]), (F[1], E[1])))
        )
        if last:
            dens_ref[0, 1] = jnp.where(eye, 0.5, 0.0) - 0.5 * node
        else:
            state[0, 0] = node
            pack(step + 1, DIAG, node)
            send_late(step + 1, DIAG)
        for q in (0, 1):
            partial[0, q] = total((A, E[q]), (D, F[q]))

        for q in (0, 1):
            v = total((DE[q], DN[q]))
            arrived(step, DDIAG, q)
            other = unpack(step, DDIAG, q)
            if first is not False:
                other = other * pick(-inverse, 1.0)
            near[1, q] = other
            put(DDN[q], other)
            u = total((E[q], DDN[q]))
            put(U[q], u + v)
            put(V[q], u + 2.0 * v)
        dnode = 1.5 * state[1, 0] - 0.5 * sym(
            total((DD, T), (D, DT), turned=((V[0], E[0]), (V[1], E[1])))
        )
        if last:
            resp_ref[0, 1] = (-0.5 * bound) * dnode
        else:
            state[1, 0] = dnode
            pack(step + 1, DDIAG, dnode)
            send_late(step + 1, DDIAG)
        for q in (0, 1):
            partial[1, q] = total((DA, E[q]), (A, DE[q]), (DD, F[q]), (D, U[q]))

        for q in (0, 1):
            arrived(step, SQUARE, q)
            other = unpack(step, SQUARE, q)
            if first is not False:
                g = shift(q)
                other = (
                    other * pick(second, 1.0)
                    + pick(4.0 * g, 0.0) * near[0, q]
                    - jnp.where(eye, pick(2.0 * g * g, 0.0), 0.0)
                )
            put(AN[q], other)
            edge = 1.5 * state[0, 1 + q] - 0.25 * (partial[0, q] + total((E[q], AN[q])))
            if last:
                dens_ref[0, place[q]] = -0.5 * edge
            else:
                state[0, 1 + q] = edge
                put(NEW[q], edge)
        if not last:
            put(D, 2.0 * state[0, 0])
            twice = total((D, D))
            wings = total(turned=((NEW[0], NEW[0]), (NEW[1], NEW[1])))
            square = 0.5 * twice + wings
            pack(step + 1, SQUARE, square)
            send_late(step + 1, SQUARE)
            put(A, square)
            put(T, 0.125 * twice + wings)
        for q in (0, 1):
            partial[1, q] += total((DE[q], AN[q]))

        for q in (0, 1):
            arrived(step, DSQUARE, q)
            other = unpack(step, DSQUARE, q)
            if first is not False:
                other = other * pick(second, 1.0) + pick(4.0 * shift(q), 0.0) * near[1, q]
            put(DAN[q], other)
            dedge = 1.5 * state[1, 1 + q] - 0.25 * (partial[1, q] + total((E[q], DAN[q])))
            if last:
                resp_ref[0, place[q]] = (-0.5 * bound) * dedge
            else:
                state[1, 1 + q] = dedge
                put(DE[q], dedge)
        if not last:
            put(DD, 2.0 * state[1, 0])
            for q in (0, 1):
                split[E[q]] = split[NEW[q]]
            twice = total((D, DD))
            wings = total(turned=((E[0], DE[0]), (E[1], DE[1])))
            square = 0.5 * twice + wings
            square = square + square.T
            pack(step + 1, DSQUARE, square)
            send_late(step + 1, DSQUARE)
            put(DA, square)
            square = 0.125 * twice + wings
            put(DT, square + square.T)

    @pl.loop(0, ITERS - 1)
    def _(step):
        iterate(step, step == 0, False)

    iterate(ITERS - 1, False, True)

    stat_all(0, GROUP - 1).wait_send()
    stat_all(1, groups - 1).wait_send()
    for step in range(ITERS):
        for kind in range(4):
            for q in (0, 1):
                copy(step, kind, q).wait_send()


def store(dens_ref, resp_ref, dens_hbm, resp_hbm, sem):
    moves = [
        pltpu.make_async_copy(src.at[0, k], dst.at[0, k], sem.at[which, k])
        for which, (src, dst) in enumerate(((dens_ref, dens_hbm), (resp_ref, resp_hbm)))
        for k in range(3)
    ]
    for move in moves:
        move.start()
    for move in moves:
        move.wait()


def per_device(n, ham, pert):
    b = ham.shape[-1]
    packed = (b + 8, b // 2)
    count = max(GROUP, n // GROUP)
    out = pl.pallas_call(
        functools.partial(kernel, n),
        out_shape=(jax.ShapeDtypeStruct(ham.shape, F32), jax.ShapeDtypeStruct(ham.shape, F32)),
        in_specs=[pl.BlockSpec(memory_space=pltpu.HBM)] * 2,
        out_specs=[pl.BlockSpec(memory_space=pltpu.VMEM)] * 2,
        scratch_shapes=[
            pltpu.VMEM(ham.shape, F32),
            pltpu.VMEM(pert.shape, F32),
            pltpu.VMEM((SLOTS, 2, b, b), BF16),
            pltpu.VMEM((2, 3, b, b), F32),
            pltpu.VMEM((2, 2, b, b), F32),
            pltpu.VMEM((4, b, b), F32),
            pltpu.VMEM((2, 2, b, b), F32),
            pltpu.VMEM((ITERS, 4) + packed, F32),
            pltpu.VMEM((ITERS, 4, 2) + packed, F32),
            pltpu.VMEM((2, 1, 128), F32),
            pltpu.VMEM((2, count, 1, 128), F32),
            pltpu.SemaphoreType.DMA((2, 3)),
            pltpu.SemaphoreType.DMA((ITERS, 4, 2)),
            pltpu.SemaphoreType.DMA((ITERS, 4, 2)),
            pltpu.SemaphoreType.DMA((2,)),
            pltpu.SemaphoreType.DMA((2,)),
            pltpu.SemaphoreType.REGULAR,
            pltpu.SemaphoreType.REGULAR,
        ],
        compiler_params=pltpu.CompilerParams(
            collective_id=0, has_side_effects=True, vmem_limit_bytes=52 * 1024 * 1024
        ),
    )(ham, pert)
    return pl.pallas_call(
        store,
        out_shape=(jax.ShapeDtypeStruct(ham.shape, F32), jax.ShapeDtypeStruct(ham.shape, F32)),
        in_specs=[pl.BlockSpec(memory_space=pl.ANY)] * 2,
        out_specs=[pl.BlockSpec(memory_space=pltpu.HBM)] * 2,
        scratch_shapes=[pltpu.SemaphoreType.DMA((2, 3))],
        compiler_params=pltpu.CompilerParams(vmem_limit_bytes=1024 * 1024),
    )(*out)


def solution(mesh):
    n = mesh.shape["chain"]
    spec = P("chain", None, None, None)
    return jax.shard_map(
        functools.partial(per_device, n),
        mesh=mesh,
        in_specs=(spec, spec),
        out_specs=(spec, spec),
        check_vma=False,
    )
```

```python
import functools

import jax
import jax.numpy as jnp
from jax import lax
from jax.experimental import pallas as pl
from jax.experimental.pallas import tpu as pltpu
from jax.sharding import PartitionSpec as P

ITERS = 3
AHEAD = ((2,), (), (1, 2), (2,))
AHEAD_ENDS = ((2,), (2,), (2,), (2,))
GROUP = 8
F32, BF16 = jnp.float32, jnp.bfloat16
MESH = pl.DeviceIdType.MESH

D, DD = 0, 1
E, DE = (2, 3), (4, 5)
DN, DDN = (6, 7), (8, 9)
AN, DAN = (10, 11), (12, 13)
A, DA, T, DT = 14, 15, 16, 17
F, U, V, W = (18, 19), (20, 21), (22, 23), (24, 25)
NEW = (26, 27)
SLOTS = 28
DIAG, DDIAG, SQUARE, DSQUARE = 0, 1, 2, 3


def halves(m):
    high = m.astype(BF16)
    return high, (m - high.astype(F32)).astype(BF16)


def whole(message):
    h = message.shape[1]
    row = lax.broadcasted_iota(jnp.int32, (h, h), 0)
    col = lax.broadcasted_iota(jnp.int32, (h, h), 1)
    off, mixed, diag = message[0:h], message[h : 2 * h], message[2 * h : 2 * h + 1]
    turned = mixed.T
    first = jnp.where(row <= col, mixed, turned)
    last = jnp.where(row > col, mixed, jnp.where(row == col, diag, turned))
    return jnp.concatenate(
        [jnp.concatenate([first, off], axis=1), jnp.concatenate([off.T, last], axis=1)], axis=0
    )


def kernel(n, ham_hbm, pert_hbm, dens_ref, resp_ref, edge_ref, late_ref, ham_ref, pert_ref, split, state, near,
           raw, partial, outbox, inbox, stat_out, stat_in, load_sem, send_sem, recv_sem,
           stat_send, stat_recv, ring_sem, late_sem):
    b = ham_hbm.shape[-1]
    h = b // 2
    groups = n // GROUP
    me = lax.axis_index("chain")
    group, local = me // GROUP, lax.rem(me, GROUP)
    inner = jnp.logical_and(local != 0, local != GROUP - 1)
    ring_low = jnp.logical_or(me == 0, jnp.logical_and(local == GROUP - 1, me != n - 1))
    ring_high = jnp.logical_or(me == n - 1, jnp.logical_and(local == 0, me != 0))
    soon = 2 * me < n
    ends = jnp.logical_or(me == 0, me == n - 1)
    middle = jnp.logical_not(jnp.logical_or(inner, ends))
    odd = lax.rem(me, 2)
    sides = (me + 1 - 2 * odd, lax.rem(me - 1 + 2 * odd + n, n))
    place = (2 - 2 * odd, 2 * odd)

    def load(which, k):
        src, dst = ((ham_hbm, ham_ref), (pert_hbm, pert_ref))[which]
        return pltpu.make_async_copy(src.at[0, k], dst.at[0, k], load_sem.at[which, k])

    for which, k in ((0, 1), (1, 1), (0, 0), (0, 2), (1, 0), (1, 2)):
        load(which, k).start()

    def signal(sem, other):
        pl.semaphore_signal(sem, inc=1, device_id=(other,), device_id_type=MESH)

    barrier = pltpu.get_barrier_semaphore()
    for off in range(1, GROUP):
        signal(barrier, group * GROUP + lax.rem(local + off, GROUP))

    @pl.loop(group + 1, groups)
    def _(other):
        signal(barrier, other * GROUP + local)

    @pl.when(ring_low)
    def _():
        signal(barrier, sides[1])

    row_h = lax.broadcasted_iota(jnp.int32, (h, h), 0)
    col_h = lax.broadcasted_iota(jnp.int32, (h, h), 1)
    row_b = lax.broadcasted_iota(jnp.int32, (b, b), 0)
    col_b = lax.broadcasted_iota(jnp.int32, (b, b), 1)
    eye = row_b == col_b

    def pack(step, kind, m):
        corner = m[h:, h:]
        outbox[step, kind, 0:h] = m[:h, h:]
        outbox[step, kind, h : 2 * h] = jnp.where(row_h <= col_h, m[:h, :h], corner)
        diag = jnp.sum(jnp.where(row_h == col_h, corner, 0.0), axis=0, keepdims=True)
        outbox[step, kind, 2 * h : 2 * h + 8] = jnp.broadcast_to(diag, (8, h))

    def unpack(step, kind, q):
        return whole(inbox.at[step, kind, q])

    def copy(step, kind, q):
        return pltpu.make_async_remote_copy(
            src_ref=outbox.at[step, kind, pl.ds(0, 2 * h + 2)],
            dst_ref=inbox.at[step, kind, q, pl.ds(0, 2 * h + 2)],
            send_sem=send_sem.at[step, kind, q],
            recv_sem=recv_sem.at[step, kind, q],
            device_id=(sides[q],),
            device_id_type=MESH,
        )

    def send(step, kind):
        for q in (1, 0):
            copy(step, kind, q).start()

    def send_late(step, kind):
        @pl.when(inner)
        def _():
            copy(step, kind, 1).start()

        copy(step, kind, 0).start()

    def follow(step, kind, ahead, which):
        step, kind = step + (kind + ahead) // 4, (kind + ahead) % 4
        valid = jnp.logical_and(step > 0, step < ITERS)

        @pl.when(jnp.logical_and(which, valid))
        def _():
            copy(jnp.minimum(step, ITERS - 1), kind, 1).start()

    def arrived(step, kind, q):
        copy(step, kind, q).wait_recv()
        if q == 0:
            for ahead in AHEAD[kind]:
                follow(step, kind, ahead, middle)
            for ahead in AHEAD_ENDS[kind]:
                follow(step, kind, ahead, ends)

    def put(slot, m):
        split[slot, 0], split[slot, 1] = halves(m)

    def product(a, c, turned):
        dims = (((1,), (1 if turned else 0,)), ((), ()))
        out = None
        for u, v in ((0, 0), (0, 1), (1, 0)):
            part = lax.dot_general(split[a, u], split[c, v], dims, preferred_element_type=F32)
            out = part if out is None else out + part
        return out

    def total(*terms, turned=()):
        out = None
        for flag, group in ((False, terms), (True, turned)):
            for a, c in group:
                part = product(a, c, flag)
                out = part if out is None else out + part
        return out

    def sym(m):
        return 0.5 * (m + m.T)

    lane = lax.broadcasted_iota(jnp.int32, (1, 128), 1)

    def stat_copy(stage, mine, other):
        return pltpu.make_async_remote_copy(
            src_ref=stat_out.at[stage],
            dst_ref=stat_in.at[stage, mine],
            send_sem=stat_send.at[stage],
            recv_sem=stat_recv.at[stage],
            device_id=(other,),
            device_id_type=MESH,
        )

    def stat_all(stage, count):
        rows = stat_in.at[stage, pl.ds(0, count)]
        return pltpu.make_async_remote_copy(
            src_ref=rows,
            dst_ref=rows,
            send_sem=stat_send.at[stage],
            recv_sem=stat_recv.at[stage],
            device_id=(sides[0],),
            device_id_type=MESH,
        )

    def merged(stage, count):
        stats = stat_in[stage, 0:count].reshape(count, 128)
        return jnp.where(
            lane == 0,
            jnp.sum(stats, axis=0, keepdims=True),
            jnp.max(stats, axis=0, keepdims=True),
        )

    load(0, 1).wait()
    centre = ham_ref[0, 1]
    pack(0, DIAG, centre)
    load(0, 0).wait()
    load(0, 2).wait()
    onsite = jnp.sum(jnp.where(eye, centre, 0.0), axis=1, keepdims=True)
    reach = jnp.sum(
        jnp.abs(ham_ref[0, 0]) + jnp.abs(centre) + jnp.abs(ham_ref[0, 2]), axis=1, keepdims=True
    ) - jnp.abs(onsite)
    level = jnp.sum(onsite, axis=0, keepdims=True)
    mine = jnp.where(
        lane == 0,
        level,
        jnp.where(
            lane == 1,
            jnp.max(onsite + reach, axis=0, keepdims=True),
            jnp.max(reach - onsite, axis=0, keepdims=True),
        ),
    )
    stat_out[0] = mine
    stat_in[0, local] = mine
    level = level / b
    load(1, 1).wait()
    pack(0, DDIAG, pert_ref[0, 1])
    pl.semaphore_wait(barrier, GROUP - 1 + group + ring_high.astype(jnp.int32))

    @pl.loop(0, group)
    def _(other):
        signal(late_sem, other * GROUP + local)

    @pl.when(ring_high)
    def _():
        signal(ring_sem, sides[1])

    for off in range(1, GROUP):
        stat_copy(0, local, group * GROUP + lax.rem(local + off, GROUP)).start()

    @pl.when(inner)
    def _():
        copy(0, DIAG, 1).start()

    copy(0, DIAG, 0).start()

    @pl.when(jnp.logical_and(inner, soon))
    def _():
        send(0, DDIAG)

    put(D, 2.0 * (centre - jnp.where(eye, level, 0.0)))
    for q in (0, 1):
        put(E[q], ham_ref[0, place[q]])
    twice = total((D, D))
    wings = total(turned=((E[0], E[0]), (E[1], E[1])))
    square = 0.5 * twice + wings
    pack(0, SQUARE, square)
    outbox[0, SQUARE, 2 * h + 1 : 2 * h + 2] = jnp.broadcast_to(level, (1, h))
    raw[0] = square
    raw[1] = 0.125 * twice + wings

    stat_all(0, GROUP - 1).wait_recv()
    mine = merged(0, GROUP)
    stat_out[1] = mine
    stat_in[1, group] = mine

    @pl.when(group < groups - 1)
    def _():
        pl.semaphore_wait(late_sem, groups - 1 - group)

    @pl.loop(1, groups)
    def _(off):
        stat_copy(1, group, lax.rem(group + off, groups) * GROUP + local).start()

    @pl.when(ring_low)
    def _():
        pl.semaphore_wait(ring_sem, 1)

    @pl.when(jnp.logical_not(inner))
    def _():
        copy(0, DIAG, 1).start()

    @pl.when(jnp.logical_not(jnp.logical_and(inner, soon)))
    def _():
        send(0, DDIAG)

    send(0, SQUARE)
    load(1, 0).wait()
    load(1, 2).wait()
    put(DD, 2.0 * pert_ref[0, 1])
    for q in (0, 1):
        put(DE[q], pert_ref[0, place[q]])
    twice = total((D, DD))
    wings = total(turned=((E[0], DE[0]), (E[1], DE[1])))
    square = 0.5 * twice + wings
    square = square + square.T
    pack(0, DSQUARE, square)
    send(0, DSQUARE)
    raw[2] = square
    square = 0.125 * twice + wings
    raw[3] = square + square.T
    stat_all(1, groups - 1).wait_recv()
    stats = merged(1, groups)
    energy = stats[:, 0:1] / (n * b)
    bound = jnp.maximum(stats[:, 1:2] - energy, energy + stats[:, 2:3]) + 1e-6
    inverse = 1.0 / bound
    second = inverse * inverse

    g = (energy - level) * inverse
    node = (jnp.where(eye, energy, 0.0) - ham_ref[0, 1]) * inverse
    dnode = -pert_ref[0, 1] * inverse
    state[0, 0] = node
    state[1, 0] = dnode
    put(D, 2.0 * node)
    put(DD, 2.0 * dnode)
    for q in (0, 1):
        edge, dedge = -ham_ref[0, place[q]] * inverse, -pert_ref[0, place[q]] * inverse
        state[0, 1 + q] = edge
        state[1, 1 + q] = dedge
        put(E[q], edge)
        put(DE[q], dedge)
    put(A, raw[0] * second + (4.0 * g) * node - jnp.where(eye, 2.0 * g * g, 0.0))
    put(T, raw[1] * second + g * node - jnp.where(eye, 0.5 * g * g, 0.0))
    put(DA, raw[2] * second + (4.0 * g) * dnode)
    put(DT, raw[3] * second + g * dnode)

    def iterate(step, first, last):
        def pick(yes, no):
            return no if first is False else jnp.where(first, yes, no)

        def shift(q):
            return (energy - inbox[0, SQUARE, q, 2 * h + 1 : 2 * h + 2, 0:1]) * inverse

        for q in (0, 1):
            arrived(step, DIAG, q)
            other = unpack(step, DIAG, q)
            if first is not False:
                other = other * pick(-inverse, 1.0) + jnp.where(eye, pick(energy * inverse, 0.0), 0.0)
            near[0, q] = other
            put(DN[q], other)
            put(F[q], total((E[q], DN[q])))
        node = 1.5 * state[0, 0] - 0.5 * sym(
            total((D, T), turned=((F[0], E[0]), (F[1], E[1])))
        )
        if last:
            dens_ref[0, 1] = jnp.where(eye, 0.5, 0.0) - 0.5 * node
        else:
            state[0, 0] = node
            pack(step + 1, DIAG, node)
            send_late(step + 1, DIAG)
        for q in (0, 1):
            partial[0, q] = total((A, E[q]), (D, F[q]))

        for q in (0, 1):
            v = total((DE[q], DN[q]))
            arrived(step, DDIAG, q)
            other = unpack(step, DDIAG, q)
            if first is not False:
                other = other * pick(-inverse, 1.0)
            near[1, q] = other
            put(DDN[q], other)
            u = total((E[q], DDN[q]))
            put(U[q], u + v)
            put(V[q], u + 2.0 * v)
        dnode = 1.5 * state[1, 0] - 0.5 * sym(
            total((DD, T), (D, DT), turned=((V[0], E[0]), (V[1], E[1])))
        )
        if last:
            resp_ref[0, 1] = (-0.5 * bound) * dnode
        else:
            state[1, 0] = dnode
            pack(step + 1, DDIAG, dnode)
            send_late(step + 1, DDIAG)
        for q in (0, 1):
            partial[1, q] = total((DA, E[q]), (A, DE[q]), (DD, F[q]), (D, U[q]))

        for q in (0, 1):
            arrived(step, SQUARE, q)
            other = unpack(step, SQUARE, q)
            if first is not False:
                g = shift(q)
                other = (
                    other * pick(second, 1.0)
                    + pick(4.0 * g, 0.0) * near[0, q]
                    - jnp.where(eye, pick(2.0 * g * g, 0.0), 0.0)
                )
            put(AN[q], other)
            edge = 1.5 * state[0, 1 + q] - 0.25 * (partial[0, q] + total((E[q], AN[q])))
            if last:
                dens_ref[0, place[q]] = -0.5 * edge
            else:
                state[0, 1 + q] = edge
                put(NEW[q], edge)
        if not last:
            put(D, 2.0 * state[0, 0])
            twice = total((D, D))
            wings = total(turned=((NEW[0], NEW[0]), (NEW[1], NEW[1])))
            square = 0.5 * twice + wings
            pack(step + 1, SQUARE, square)
            send_late(step + 1, SQUARE)
            put(A, square)
            put(T, 0.125 * twice + wings)
        for q in (0, 1):
            partial[1, q] += total((DE[q], AN[q]))

        if last:
            resp_ref[0, place[1]] = (-0.5 * bound) * (1.5 * state[1, 2] - 0.25 * partial[1, 1])
            edge_ref[0], edge_ref[1] = halves((0.125 * bound) * state[0, 2])
        for q in (0, 1):
            arrived(step, DSQUARE, q)
            if last and q == 1:
                late_ref[...] = inbox[step, DSQUARE, 1, 0 : 2 * h + 1]
                continue
            other = unpack(step, DSQUARE, q)
            if first is not False:
                other = other * pick(second, 1.0) + pick(4.0 * shift(q), 0.0) * near[1, q]
            put(DAN[q], other)
            dedge = 1.5 * state[1, 1 + q] - 0.25 * (partial[1, q] + total((E[q], DAN[q])))
            if last:
                resp_ref[0, place[q]] = (-0.5 * bound) * dedge
            else:
                state[1, 1 + q] = dedge
                put(DE[q], dedge)
        if not last:
            put(DD, 2.0 * state[1, 0])
            for q in (0, 1):
                split[E[q]] = split[NEW[q]]
            twice = total((D, DD))
            wings = total(turned=((E[0], DE[0]), (E[1], DE[1])))
            square = 0.5 * twice + wings
            square = square + square.T
            pack(step + 1, DSQUARE, square)
            send_late(step + 1, DSQUARE)
            put(DA, square)
            square = 0.125 * twice + wings
            put(DT, square + square.T)

    @pl.loop(0, ITERS - 1)
    def _(step):
        iterate(step, step == 0, False)

    iterate(ITERS - 1, False, True)

    stat_all(0, GROUP - 1).wait_send()
    stat_all(1, groups - 1).wait_send()
    for step in range(ITERS):
        for kind in range(4):
            for q in (0, 1):
                copy(step, kind, q).wait_send()


def store(dens_ref, resp_ref, edge_ref, late_ref, dens_hbm, resp_hbm, done, sem):
    late = 2 * lax.rem(lax.axis_index("chain"), 2)
    moves = [pltpu.make_async_copy(dens_ref.at[0, k], dens_hbm.at[0, k], sem.at[k]) for k in range(3)]
    for at, k in ((3, 1), (4, 2 - late)):
        moves.append(pltpu.make_async_copy(resp_ref.at[0, k], resp_hbm.at[0, k], sem.at[at]))
    for move in moves:
        move.start()
    high, low = halves(whole(late_ref))
    out = resp_ref[0, late]
    for a, c in ((edge_ref[0], high), (edge_ref[0], low), (edge_ref[1], high)):
        out += jnp.dot(a, c, preferred_element_type=F32)
    done[...] = out
    moves.append(pltpu.make_async_copy(done, resp_hbm.at[0, late], sem.at[5]))
    moves[-1].start()
    for move in moves:
        move.wait()


def per_device(n, ham, pert):
    b = ham.shape[-1]
    packed = (b + 8, b // 2)
    count = max(GROUP, n // GROUP)
    out = pl.pallas_call(
        functools.partial(kernel, n),
        out_shape=(
            jax.ShapeDtypeStruct(ham.shape, F32),
            jax.ShapeDtypeStruct(ham.shape, F32),
            jax.ShapeDtypeStruct((2, b, b), BF16),
            jax.ShapeDtypeStruct((b + 1, b // 2), F32),
        ),
        in_specs=[pl.BlockSpec(memory_space=pltpu.HBM)] * 2,
        out_specs=[pl.BlockSpec(memory_space=pltpu.VMEM)] * 4,
        scratch_shapes=[
            pltpu.VMEM(ham.shape, F32),
            pltpu.VMEM(pert.shape, F32),
            pltpu.VMEM((SLOTS, 2, b, b), BF16),
            pltpu.VMEM((2, 3, b, b), F32),
            pltpu.VMEM((2, 2, b, b), F32),
            pltpu.VMEM((4, b, b), F32),
            pltpu.VMEM((2, 2, b, b), F32),
            pltpu.VMEM((ITERS, 4) + packed, F32),
            pltpu.VMEM((ITERS, 4, 2) + packed, F32),
            pltpu.VMEM((2, 1, 128), F32),
            pltpu.VMEM((2, count, 1, 128), F32),
            pltpu.SemaphoreType.DMA((2, 3)),
            pltpu.SemaphoreType.DMA((ITERS, 4, 2)),
            pltpu.SemaphoreType.DMA((ITERS, 4, 2)),
            pltpu.SemaphoreType.DMA((2,)),
            pltpu.SemaphoreType.DMA((2,)),
            pltpu.SemaphoreType.REGULAR,
            pltpu.SemaphoreType.REGULAR,
        ],
        compiler_params=pltpu.CompilerParams(
            collective_id=0, has_side_effects=True, vmem_limit_bytes=52 * 1024 * 1024
        ),
    )(ham, pert)
    return pl.pallas_call(
        store,
        out_shape=(jax.ShapeDtypeStruct(ham.shape, F32), jax.ShapeDtypeStruct(ham.shape, F32)),
        in_specs=[pl.BlockSpec(memory_space=pltpu.VMEM)] * 4,
        out_specs=[pl.BlockSpec(memory_space=pltpu.HBM)] * 2,
        scratch_shapes=[pltpu.VMEM((b, b), F32), pltpu.SemaphoreType.DMA((6,))],
        compiler_params=pltpu.CompilerParams(vmem_limit_bytes=4 * 1024 * 1024),
    )(*out)


def solution(mesh):
    n = mesh.shape["chain"]
    spec = P("chain", None, None, None)
    return jax.shard_map(
        functools.partial(per_device, n),
        mesh=mesh,
        in_specs=(spec, spec),
        out_specs=(spec, spec),
        check_vma=False,
    )
```

```python
import functools

import jax
import jax.numpy as jnp
from jax import lax
from jax.experimental import pallas as pl
from jax.experimental.pallas import tpu as pltpu
from jax.sharding import PartitionSpec as P

ITERS = 3
AHEAD = ((2,), (), (1, 2), (2,))
AHEAD_ENDS = ((2,), (2,), (2,), (2,))
GROUP = 8
F32, BF16 = jnp.float32, jnp.bfloat16
MESH = pl.DeviceIdType.MESH

D, DD = 0, 1
E, DE = (2, 3), (4, 5)
DN, DDN = (6, 7), (8, 9)
AN, DAN = (10, 11), (12, 13)
A, DA, T, DT = 14, 15, 16, 17
F, U, V, W = (18, 19), (20, 21), (22, 23), (24, 25)
NEW = (26, 27)
SLOTS = 28
DIAG, DDIAG, SQUARE, DSQUARE = 0, 1, 2, 3


def halves(m):
    high = m.astype(BF16)
    return high, (m - high.astype(F32)).astype(BF16)


def whole(message):
    h = message.shape[1]
    row = lax.broadcasted_iota(jnp.int32, (h, h), 0)
    col = lax.broadcasted_iota(jnp.int32, (h, h), 1)
    off, mixed, diag = message[0:h], message[h : 2 * h], message[2 * h : 2 * h + 1]
    turned = mixed.T
    first = jnp.where(row <= col, mixed, turned)
    last = jnp.where(row > col, mixed, jnp.where(row == col, diag, turned))
    return jnp.concatenate(
        [jnp.concatenate([first, off], axis=1), jnp.concatenate([off.T, last], axis=1)], axis=0
    )


def kernel(n, ham_hbm, pert_hbm, dens_ref, resp_ref, edge_ref, late_ref, ham_ref, pert_ref, split, state, near,
           raw, partial, outbox, inbox, stat_out, stat_in, load_sem, send_sem, recv_sem,
           stat_send, stat_recv, ring_sem, late_sem):
    b = ham_hbm.shape[-1]
    h = b // 2
    groups = n // GROUP
    me = lax.axis_index("chain")
    group, local = me // GROUP, lax.rem(me, GROUP)
    inner = jnp.logical_and(local != 0, local != GROUP - 1)
    ring_low = jnp.logical_or(me == 0, jnp.logical_and(local == GROUP - 1, me != n - 1))
    ring_high = jnp.logical_or(me == n - 1, jnp.logical_and(local == 0, me != 0))
    soon = 4 * me < n
    ends = jnp.logical_or(me == 0, me == n - 1)
    middle = jnp.logical_not(jnp.logical_or(inner, ends))
    odd = lax.rem(me, 2)
    sides = (me + 1 - 2 * odd, lax.rem(me - 1 + 2 * odd + n, n))
    place = (2 - 2 * odd, 2 * odd)

    def load(which, k):
        src, dst = ((ham_hbm, ham_ref), (pert_hbm, pert_ref))[which]
        return pltpu.make_async_copy(src.at[0, k], dst.at[0, k], load_sem.at[which, k])

    for which, k in ((0, 1), (1, 1), (0, 0), (0, 2), (1, 0), (1, 2)):
        load(which, k).start()

    def signal(sem, other):
        pl.semaphore_signal(sem, inc=1, device_id=(other,), device_id_type=MESH)

    barrier = pltpu.get_barrier_semaphore()
    for off in range(1, GROUP):
        signal(barrier, group * GROUP + lax.rem(local + off, GROUP))

    @pl.loop(group + 1, groups)
    def _(other):
        signal(barrier, other * GROUP + local)

    @pl.when(ring_low)
    def _():
        signal(barrier, sides[1])

    row_h = lax.broadcasted_iota(jnp.int32, (h, h), 0)
    col_h = lax.broadcasted_iota(jnp.int32, (h, h), 1)
    row_b = lax.broadcasted_iota(jnp.int32, (b, b), 0)
    col_b = lax.broadcasted_iota(jnp.int32, (b, b), 1)
    eye = row_b == col_b

    def pack(step, kind, m):
        corner = m[h:, h:]
        outbox[step, kind, 0:h] = m[:h, h:]
        outbox[step, kind, h : 2 * h] = jnp.where(row_h <= col_h, m[:h, :h], corner)
        diag = jnp.sum(jnp.where(row_h == col_h, corner, 0.0), axis=0, keepdims=True)
        outbox[step, kind, 2 * h : 2 * h + 8] = jnp.broadcast_to(diag, (8, h))

    def unpack(step, kind, q):
        return whole(inbox.at[step, kind, q])

    def copy(step, kind, q):
        return pltpu.make_async_remote_copy(
            src_ref=outbox.at[step, kind, pl.ds(0, 2 * h + 2)],
            dst_ref=inbox.at[step, kind, q, pl.ds(0, 2 * h + 2)],
            send_sem=send_sem.at[step, kind, q],
            recv_sem=recv_sem.at[step, kind, q],
            device_id=(sides[q],),
            device_id_type=MESH,
        )

    def send(step, kind):
        for q in (1, 0):
            copy(step, kind, q).start()

    def send_late(step, kind):
        @pl.when(inner)
        def _():
            copy(step, kind, 1).start()

        copy(step, kind, 0).start()

    def follow(step, kind, ahead, which):
        step, kind = step + (kind + ahead) // 4, (kind + ahead) % 4
        valid = jnp.logical_and(step > 0, step < ITERS)

        @pl.when(jnp.logical_and(which, valid))
        def _():
            copy(jnp.minimum(step, ITERS - 1), kind, 1).start()

    def arrived(step, kind, q):
        copy(step, kind, q).wait_recv()
        if q == 0:
            for ahead in AHEAD[kind]:
                follow(step, kind, ahead, middle)
            for ahead in AHEAD_ENDS[kind]:
                follow(step, kind, ahead, ends)

    def put(slot, m):
        split[slot, 0], split[slot, 1] = halves(m)

    def product(a, c, turned):
        dims = (((1,), (1 if turned else 0,)), ((), ()))
        out = None
        for u, v in ((0, 0), (0, 1), (1, 0)):
            part = lax.dot_general(split[a, u], split[c, v], dims, preferred_element_type=F32)
            out = part if out is None else out + part
        return out

    def total(*terms, turned=()):
        out = None
        for flag, group in ((False, terms), (True, turned)):
            for a, c in group:
                part = product(a, c, flag)
                out = part if out is None else out + part
        return out

    def sym(m):
        return 0.5 * (m + m.T)

    lane = lax.broadcasted_iota(jnp.int32, (1, 128), 1)

    def stat_copy(stage, mine, other):
        return pltpu.make_async_remote_copy(
            src_ref=stat_out.at[stage],
            dst_ref=stat_in.at[stage, mine],
            send_sem=stat_send.at[stage],
            recv_sem=stat_recv.at[stage],
            device_id=(other,),
            device_id_type=MESH,
        )

    def stat_all(stage, count):
        rows = stat_in.at[stage, pl.ds(0, count)]
        return pltpu.make_async_remote_copy(
            src_ref=rows,
            dst_ref=rows,
            send_sem=stat_send.at[stage],
            recv_sem=stat_recv.at[stage],
            device_id=(sides[0],),
            device_id_type=MESH,
        )

    def merged(stage, count):
        stats = stat_in[stage, 0:count].reshape(count, 128)
        return jnp.where(
            lane == 0,
            jnp.sum(stats, axis=0, keepdims=True),
            jnp.max(stats, axis=0, keepdims=True),
        )

    load(0, 1).wait()
    centre = ham_ref[0, 1]
    pack(0, DIAG, centre)
    load(0, 0).wait()
    load(0, 2).wait()
    onsite = jnp.sum(jnp.where(eye, centre, 0.0), axis=1, keepdims=True)
    reach = jnp.sum(
        jnp.abs(ham_ref[0, 0]) + jnp.abs(centre) + jnp.abs(ham_ref[0, 2]), axis=1, keepdims=True
    ) - jnp.abs(onsite)
    level = jnp.sum(onsite, axis=0, keepdims=True)
    mine = jnp.where(
        lane == 0,
        level,
        jnp.where(
            lane == 1,
            jnp.max(onsite + reach, axis=0, keepdims=True),
            jnp.max(reach - onsite, axis=0, keepdims=True),
        ),
    )
    stat_out[0] = mine
    stat_in[0, local] = mine
    level = level / b
    load(1, 1).wait()
    pack(0, DDIAG, pert_ref[0, 1])
    pl.semaphore_wait(barrier, GROUP - 1 + group + ring_high.astype(jnp.int32))

    @pl.loop(0, group)
    def _(other):
        signal(late_sem, other * GROUP + local)

    @pl.when(ring_high)
    def _():
        signal(ring_sem, sides[1])

    for off in range(1, GROUP):
        stat_copy(0, local, group * GROUP + lax.rem(local + off, GROUP)).start()

    @pl.when(inner)
    def _():
        copy(0, DIAG, 1).start()

    copy(0, DIAG, 0).start()

    @pl.when(jnp.logical_and(inner, soon))
    def _():
        send(0, DDIAG)

    put(D, 2.0 * (centre - jnp.where(eye, level, 0.0)))
    for q in (0, 1):
        put(E[q], ham_ref[0, place[q]])
    twice = total((D, D))
    wings = total(turned=((E[0], E[0]), (E[1], E[1])))
    square = 0.5 * twice + wings
    pack(0, SQUARE, square)
    outbox[0, SQUARE, 2 * h + 1 : 2 * h + 2] = jnp.broadcast_to(level, (1, h))
    raw[0] = square
    raw[1] = 0.125 * twice + wings

    stat_all(0, GROUP - 1).wait_recv()
    mine = merged(0, GROUP)
    stat_out[1] = mine
    stat_in[1, group] = mine

    @pl.when(group < groups - 1)
    def _():
        pl.semaphore_wait(late_sem, groups - 1 - group)

    @pl.loop(1, groups)
    def _(off):
        stat_copy(1, group, lax.rem(group + off, groups) * GROUP + local).start()

    @pl.when(ring_low)
    def _():
        pl.semaphore_wait(ring_sem, 1)

    @pl.when(jnp.logical_not(inner))
    def _():
        copy(0, DIAG, 1).start()

    @pl.when(jnp.logical_not(jnp.logical_and(inner, soon)))
    def _():
        send(0, DDIAG)

    send(0, SQUARE)
    load(1, 0).wait()
    load(1, 2).wait()
    put(DD, 2.0 * pert_ref[0, 1])
    for q in (0, 1):
        put(DE[q], pert_ref[0, place[q]])
    twice = total((D, DD))
    wings = total(turned=((E[0], DE[0]), (E[1], DE[1])))
    square = 0.5 * twice + wings
    square = square + square.T
    pack(0, DSQUARE, square)
    send(0, DSQUARE)
    raw[2] = square
    square = 0.125 * twice + wings
    raw[3] = square + square.T
    stat_all(1, groups - 1).wait_recv()
    stats = merged(1, groups)
    energy = stats[:, 0:1] / (n * b)
    bound = jnp.maximum(stats[:, 1:2] - energy, energy + stats[:, 2:3]) + 1e-6
    inverse = 1.0 / bound
    second = inverse * inverse

    g = (energy - level) * inverse
    node = (jnp.where(eye, energy, 0.0) - ham_ref[0, 1]) * inverse
    dnode = -pert_ref[0, 1] * inverse
    state[0, 0] = node
    state[1, 0] = dnode
    put(D, 2.0 * node)
    put(DD, 2.0 * dnode)
    for q in (0, 1):
        edge, dedge = -ham_ref[0, place[q]] * inverse, -pert_ref[0, place[q]] * inverse
        state[0, 1 + q] = edge
        state[1, 1 + q] = dedge
        put(E[q], edge)
        put(DE[q], dedge)
    put(A, raw[0] * second + (4.0 * g) * node - jnp.where(eye, 2.0 * g * g, 0.0))
    put(T, raw[1] * second + g * node - jnp.where(eye, 0.5 * g * g, 0.0))
    put(DA, raw[2] * second + (4.0 * g) * dnode)
    put(DT, raw[3] * second + g * dnode)

    def iterate(step, first, last):
        def pick(yes, no):
            return no if first is False else jnp.where(first, yes, no)

        def shift(q):
            return (energy - inbox[0, SQUARE, q, 2 * h + 1 : 2 * h + 2, 0:1]) * inverse

        for q in (0, 1):
            arrived(step, DIAG, q)
            other = unpack(step, DIAG, q)
            if first is not False:
                other = other * pick(-inverse, 1.0) + jnp.where(eye, pick(energy * inverse, 0.0), 0.0)
            near[0, q] = other
            put(DN[q], other)
            put(F[q], total((E[q], DN[q])))
        node = 1.5 * state[0, 0] - 0.5 * sym(
            total((D, T), turned=((F[0], E[0]), (F[1], E[1])))
        )
        if last:
            dens_ref[0, 1] = jnp.where(eye, 0.5, 0.0) - 0.5 * node
        else:
            state[0, 0] = node
            pack(step + 1, DIAG, node)
            send_late(step + 1, DIAG)
        for q in (0, 1):
            partial[0, q] = total((A, E[q]), (D, F[q]))

        for q in (0, 1):
            v = total((DE[q], DN[q]))
            arrived(step, DDIAG, q)
            other = unpack(step, DDIAG, q)
            if first is not False:
                other = other * pick(-inverse, 1.0)
            near[1, q] = other
            put(DDN[q], other)
            u = total((E[q], DDN[q]))
            put(U[q], u + v)
            put(V[q], u + 2.0 * v)
        dnode = 1.5 * state[1, 0] - 0.5 * sym(
            total((DD, T), (D, DT), turned=((V[0], E[0]), (V[1], E[1])))
        )
        if last:
            resp_ref[0, 1] = (-0.5 * bound) * dnode
        else:
            state[1, 0] = dnode
            pack(step + 1, DDIAG, dnode)
            send_late(step + 1, DDIAG)
        for q in (0, 1):
            partial[1, q] = total((DA, E[q]), (A, DE[q]), (DD, F[q]), (D, U[q]))

        for q in (0, 1):
            arrived(step, SQUARE, q)
            other = unpack(step, SQUARE, q)
            if first is not False:
                g = shift(q)
                other = (
                    other * pick(second, 1.0)
                    + pick(4.0 * g, 0.0) * near[0, q]
                    - jnp.where(eye, pick(2.0 * g * g, 0.0), 0.0)
                )
            put(AN[q], other)
            edge = 1.5 * state[0, 1 + q] - 0.25 * (partial[0, q] + total((E[q], AN[q])))
            if last:
                dens_ref[0, place[q]] = -0.5 * edge
            else:
                state[0, 1 + q] = edge
                put(NEW[q], edge)
        if not last:
            put(D, 2.0 * state[0, 0])
            twice = total((D, D))
            wings = total(turned=((NEW[0], NEW[0]), (NEW[1], NEW[1])))
            square = 0.5 * twice + wings
            pack(step + 1, SQUARE, square)
            send_late(step + 1, SQUARE)
            put(A, square)
            put(T, 0.125 * twice + wings)
        for q in (0, 1):
            partial[1, q] += total((DE[q], AN[q]))

        if last:
            resp_ref[0, place[1]] = (-0.5 * bound) * (1.5 * state[1, 2] - 0.25 * partial[1, 1])
            edge_ref[0], edge_ref[1] = halves((0.125 * bound) * state[0, 2])
        for q in (0, 1):
            arrived(step, DSQUARE, q)
            if last and q == 1:
                late_ref[...] = inbox[step, DSQUARE, 1, 0 : 2 * h + 1]
                continue
            other = unpack(step, DSQUARE, q)
            if first is not False:
                other = other * pick(second, 1.0) + pick(4.0 * shift(q), 0.0) * near[1, q]
            put(DAN[q], other)
            dedge = 1.5 * state[1, 1 + q] - 0.25 * (partial[1, q] + total((E[q], DAN[q])))
            if last:
                resp_ref[0, place[q]] = (-0.5 * bound) * dedge
            else:
                state[1, 1 + q] = dedge
                put(DE[q], dedge)
        if not last:
            put(DD, 2.0 * state[1, 0])
            for q in (0, 1):
                split[E[q]] = split[NEW[q]]
            twice = total((D, DD))
            wings = total(turned=((E[0], DE[0]), (E[1], DE[1])))
            square = 0.5 * twice + wings
            square = square + square.T
            pack(step + 1, DSQUARE, square)
            send_late(step + 1, DSQUARE)
            put(DA, square)
            square = 0.125 * twice + wings
            put(DT, square + square.T)

    @pl.loop(0, ITERS - 1)
    def _(step):
        iterate(step, step == 0, False)

    iterate(ITERS - 1, False, True)

    stat_all(0, GROUP - 1).wait_send()
    stat_all(1, groups - 1).wait_send()
    for step in range(ITERS):
        for kind in range(4):
            for q in (0, 1):
                copy(step, kind, q).wait_send()


def store(dens_ref, resp_ref, edge_ref, late_ref, dens_hbm, resp_hbm, done, sem):
    late = 2 * lax.rem(lax.axis_index("chain"), 2)
    moves = [pltpu.make_async_copy(dens_ref.at[0, k], dens_hbm.at[0, k], sem.at[k]) for k in range(3)]
    for at, k in ((3, 1), (4, 2 - late)):
        moves.append(pltpu.make_async_copy(resp_ref.at[0, k], resp_hbm.at[0, k], sem.at[at]))
    for move in moves:
        move.start()
    high, low = halves(whole(late_ref))
    out = resp_ref[0, late]
    for a, c in ((edge_ref[0], high), (edge_ref[0], low), (edge_ref[1], high)):
        out += jnp.dot(a, c, preferred_element_type=F32)
    done[...] = out
    moves.append(pltpu.make_async_copy(done, resp_hbm.at[0, late], sem.at[5]))
    moves[-1].start()
    for move in moves:
        move.wait()


def per_device(n, ham, pert):
    b = ham.shape[-1]
    packed = (b + 8, b // 2)
    count = max(GROUP, n // GROUP)
    out = pl.pallas_call(
        functools.partial(kernel, n),
        out_shape=(
            jax.ShapeDtypeStruct(ham.shape, F32),
            jax.ShapeDtypeStruct(ham.shape, F32),
            jax.ShapeDtypeStruct((2, b, b), BF16),
            jax.ShapeDtypeStruct((b + 1, b // 2), F32),
        ),
        in_specs=[pl.BlockSpec(memory_space=pltpu.HBM)] * 2,
        out_specs=[pl.BlockSpec(memory_space=pltpu.VMEM)] * 4,
        scratch_shapes=[
            pltpu.VMEM(ham.shape, F32),
            pltpu.VMEM(pert.shape, F32),
            pltpu.VMEM((SLOTS, 2, b, b), BF16),
            pltpu.VMEM((2, 3, b, b), F32),
            pltpu.VMEM((2, 2, b, b), F32),
            pltpu.VMEM((4, b, b), F32),
            pltpu.VMEM((2, 2, b, b), F32),
            pltpu.VMEM((ITERS, 4) + packed, F32),
            pltpu.VMEM((ITERS, 4, 2) + packed, F32),
            pltpu.VMEM((2, 1, 128), F32),
            pltpu.VMEM((2, count, 1, 128), F32),
            pltpu.SemaphoreType.DMA((2, 3)),
            pltpu.SemaphoreType.DMA((ITERS, 4, 2)),
            pltpu.SemaphoreType.DMA((ITERS, 4, 2)),
            pltpu.SemaphoreType.DMA((2,)),
            pltpu.SemaphoreType.DMA((2,)),
            pltpu.SemaphoreType.REGULAR,
            pltpu.SemaphoreType.REGULAR,
        ],
        compiler_params=pltpu.CompilerParams(
            collective_id=0, has_side_effects=True, vmem_limit_bytes=52 * 1024 * 1024
        ),
    )(ham, pert)
    return pl.pallas_call(
        store,
        out_shape=(jax.ShapeDtypeStruct(ham.shape, F32), jax.ShapeDtypeStruct(ham.shape, F32)),
        in_specs=[pl.BlockSpec(memory_space=pltpu.VMEM)] * 4,
        out_specs=[pl.BlockSpec(memory_space=pltpu.HBM)] * 2,
        scratch_shapes=[pltpu.VMEM((b, b), F32), pltpu.SemaphoreType.DMA((6,))],
        compiler_params=pltpu.CompilerParams(vmem_limit_bytes=4 * 1024 * 1024),
    )(*out)


def solution(mesh):
    n = mesh.shape["chain"]
    spec = P("chain", None, None, None)
    return jax.shard_map(
        functools.partial(per_device, n),
        mesh=mesh,
        in_specs=(spec, spec),
        out_specs=(spec, spec),
        check_vma=False,
    )
```

```python
import functools

import jax
import jax.numpy as jnp
from jax import lax
from jax.experimental import pallas as pl
from jax.experimental.pallas import tpu as pltpu
from jax.sharding import PartitionSpec as P

ITERS = 3
AHEAD = ((2,), (), (1, 2), (2,))
AHEAD_ENDS = ((2,), (2,), (2,), (2,))
GROUP = 8
F32, BF16 = jnp.float32, jnp.bfloat16
MESH = pl.DeviceIdType.MESH

D, DD = 0, 1
E, DE = (2, 3), (4, 5)
DN, DDN = (6, 7), (8, 9)
AN, DAN = (10, 11), (12, 13)
A, DA, T, DT = 14, 15, 16, 17
F, U, V, W = (18, 19), (20, 21), (22, 23), (24, 25)
NEW = (26, 27)
SLOTS = 28
DIAG, DDIAG, SQUARE, DSQUARE = 0, 1, 2, 3


def halves(m):
    high = m.astype(BF16)
    return high, (m - high.astype(F32)).astype(BF16)


def whole(message):
    h = message.shape[1]
    row = lax.broadcasted_iota(jnp.int32, (h, h), 0)
    col = lax.broadcasted_iota(jnp.int32, (h, h), 1)
    off, mixed, diag = message[0:h], message[h : 2 * h], message[2 * h : 2 * h + 1]
    turned = mixed.T
    first = jnp.where(row <= col, mixed, turned)
    last = jnp.where(row > col, mixed, jnp.where(row == col, diag, turned))
    return jnp.concatenate(
        [jnp.concatenate([first, off], axis=1), jnp.concatenate([off.T, last], axis=1)], axis=0
    )


def kernel(n, ham_hbm, pert_hbm, dens_ref, resp_ref, edge_ref, late_ref, ham_ref, pert_ref, split, state, near,
           raw, partial, outbox, inbox, stat_out, stat_in, load_sem, send_sem, recv_sem,
           stat_send, stat_recv, ring_sem, late_sem):
    b = ham_hbm.shape[-1]
    h = b // 2
    groups = n // GROUP
    me = lax.axis_index("chain")
    group, local = me // GROUP, lax.rem(me, GROUP)
    inner = jnp.logical_and(local != 0, local != GROUP - 1)
    ring_low = jnp.logical_or(me == 0, jnp.logical_and(local == GROUP - 1, me != n - 1))
    ring_high = jnp.logical_or(me == n - 1, jnp.logical_and(local == 0, me != 0))
    soon = 4 * me < n
    ends = jnp.logical_or(me == 0, me == n - 1)
    middle = jnp.logical_not(jnp.logical_or(inner, ends))
    odd = lax.rem(me, 2)
    sides = (me + 1 - 2 * odd, lax.rem(me - 1 + 2 * odd + n, n))
    place = (2 - 2 * odd, 2 * odd)

    def load(which, k):
        src, dst = ((ham_hbm, ham_ref), (pert_hbm, pert_ref))[which]
        return pltpu.make_async_copy(src.at[0, k], dst.at[0, k], load_sem.at[which, k])

    for which, k in ((0, 1), (1, 1), (0, 0), (0, 2), (1, 0), (1, 2)):
        load(which, k).start()

    def signal(sem, other):
        pl.semaphore_signal(sem, inc=1, device_id=(other,), device_id_type=MESH)

    barrier = pltpu.get_barrier_semaphore()
    for off in range(1, GROUP):
        signal(barrier, group * GROUP + lax.rem(local + off, GROUP))

    @pl.loop(group + 1, groups)
    def _(other):
        signal(barrier, other * GROUP + local)

    @pl.when(ring_low)
    def _():
        signal(barrier, sides[1])

    row_h = lax.broadcasted_iota(jnp.int32, (h, h), 0)
    col_h = lax.broadcasted_iota(jnp.int32, (h, h), 1)
    row_b = lax.broadcasted_iota(jnp.int32, (b, b), 0)
    col_b = lax.broadcasted_iota(jnp.int32, (b, b), 1)
    eye = row_b == col_b

    def pack(step, kind, m):
        corner = m[h:, h:]
        outbox[step, kind, 0:h] = m[:h, h:]
        outbox[step, kind, h : 2 * h] = jnp.where(row_h <= col_h, m[:h, :h], corner)
        diag = jnp.sum(jnp.where(row_h == col_h, corner, 0.0), axis=0, keepdims=True)
        outbox[step, kind, 2 * h : 2 * h + 8] = jnp.broadcast_to(diag, (8, h))

    def unpack(step, kind, q):
        return whole(inbox.at[step, kind, q])

    def copy(step, kind, q):
        return pltpu.make_async_remote_copy(
            src_ref=outbox.at[step, kind, pl.ds(0, 2 * h + 2)],
            dst_ref=inbox.at[step, kind, q, pl.ds(0, 2 * h + 2)],
            send_sem=send_sem.at[step, kind, q],
            recv_sem=recv_sem.at[step, kind, q],
            device_id=(sides[q],),
            device_id_type=MESH,
        )

    def send(step, kind):
        for q in (1, 0):
            copy(step, kind, q).start()

    def send_late(step, kind):
        copy(step, kind, 0).start()

        @pl.when(inner)
        def _():
            copy(step, kind, 1).start()

    def follow(step, kind, ahead, which):
        step, kind = step + (kind + ahead) // 4, (kind + ahead) % 4
        valid = jnp.logical_and(step > 0, step < ITERS)

        @pl.when(jnp.logical_and(which, valid))
        def _():
            copy(jnp.minimum(step, ITERS - 1), kind, 1).start()

    def arrived(step, kind, q):
        copy(step, kind, q).wait_recv()
        if q == 0:
            for ahead in AHEAD[kind]:
                follow(step, kind, ahead, middle)
            for ahead in AHEAD_ENDS[kind]:
                follow(step, kind, ahead, ends)

    def put(slot, m):
        split[slot, 0], split[slot, 1] = halves(m)

    def product(a, c, turned):
        dims = (((1,), (1 if turned else 0,)), ((), ()))
        out = None
        for u, v in ((0, 0), (0, 1), (1, 0)):
            part = lax.dot_general(split[a, u], split[c, v], dims, preferred_element_type=F32)
            out = part if out is None else out + part
        return out

    def total(*terms, turned=()):
        out = None
        for flag, group in ((False, terms), (True, turned)):
            for a, c in group:
                part = product(a, c, flag)
                out = part if out is None else out + part
        return out

    def sym(m):
        return 0.5 * (m + m.T)

    lane = lax.broadcasted_iota(jnp.int32, (1, 128), 1)

    def stat_copy(stage, mine, other):
        return pltpu.make_async_remote_copy(
            src_ref=stat_out.at[stage],
            dst_ref=stat_in.at[stage, mine],
            send_sem=stat_send.at[stage],
            recv_sem=stat_recv.at[stage],
            device_id=(other,),
            device_id_type=MESH,
        )

    def stat_all(stage, count):
        rows = stat_in.at[stage, pl.ds(0, count)]
        return pltpu.make_async_remote_copy(
            src_ref=rows,
            dst_ref=rows,
            send_sem=stat_send.at[stage],
            recv_sem=stat_recv.at[stage],
            device_id=(sides[0],),
            device_id_type=MESH,
        )

    def merged(stage, count):
        stats = stat_in[stage, 0:count].reshape(count, 128)
        return jnp.where(
            lane == 0,
            jnp.sum(stats, axis=0, keepdims=True),
            jnp.max(stats, axis=0, keepdims=True),
        )

    load(0, 1).wait()
    centre = ham_ref[0, 1]
    pack(0, DIAG, centre)
    load(0, 0).wait()
    load(0, 2).wait()
    onsite = jnp.sum(jnp.where(eye, centre, 0.0), axis=1, keepdims=True)
    reach = jnp.sum(
        jnp.abs(ham_ref[0, 0]) + jnp.abs(centre) + jnp.abs(ham_ref[0, 2]), axis=1, keepdims=True
    ) - jnp.abs(onsite)
    level = jnp.sum(onsite, axis=0, keepdims=True)
    mine = jnp.where(
        lane == 0,
        level,
        jnp.where(
            lane == 1,
            jnp.max(onsite + reach, axis=0, keepdims=True),
            jnp.max(reach - onsite, axis=0, keepdims=True),
        ),
    )
    stat_out[0] = mine
    stat_in[0, local] = mine
    level = level / b
    load(1, 1).wait()
    pack(0, DDIAG, pert_ref[0, 1])
    pl.semaphore_wait(barrier, GROUP - 1 + group + ring_high.astype(jnp.int32))

    @pl.loop(0, group)
    def _(other):
        signal(late_sem, other * GROUP + local)

    @pl.when(ring_high)
    def _():
        signal(ring_sem, sides[1])

    for off in range(1, GROUP):
        stat_copy(0, local, group * GROUP + lax.rem(local + off, GROUP)).start()

    @pl.when(inner)
    def _():
        copy(0, DIAG, 1).start()

    copy(0, DIAG, 0).start()

    @pl.when(jnp.logical_and(inner, soon))
    def _():
        send(0, DDIAG)

    put(D, 2.0 * (centre - jnp.where(eye, level, 0.0)))
    for q in (0, 1):
        put(E[q], ham_ref[0, place[q]])
    twice = total((D, D))
    wings = total(turned=((E[0], E[0]), (E[1], E[1])))
    square = 0.5 * twice + wings
    pack(0, SQUARE, square)
    outbox[0, SQUARE, 2 * h + 1 : 2 * h + 2] = jnp.broadcast_to(level, (1, h))
    raw[0] = square
    raw[1] = 0.125 * twice + wings

    stat_all(0, GROUP - 1).wait_recv()
    mine = merged(0, GROUP)
    stat_out[1] = mine
    stat_in[1, group] = mine

    @pl.when(group < groups - 1)
    def _():
        pl.semaphore_wait(late_sem, groups - 1 - group)

    @pl.loop(1, groups)
    def _(off):
        stat_copy(1, group, lax.rem(group + off, groups) * GROUP + local).start()

    @pl.when(ring_low)
    def _():
        pl.semaphore_wait(ring_sem, 1)

    @pl.when(jnp.logical_not(inner))
    def _():
        copy(0, DIAG, 1).start()

    @pl.when(jnp.logical_not(jnp.logical_and(inner, soon)))
    def _():
        send(0, DDIAG)

    send(0, SQUARE)
    load(1, 0).wait()
    load(1, 2).wait()
    put(DD, 2.0 * pert_ref[0, 1])
    for q in (0, 1):
        put(DE[q], pert_ref[0, place[q]])
    twice = total((D, DD))
    wings = total(turned=((E[0], DE[0]), (E[1], DE[1])))
    square = 0.5 * twice + wings
    square = square + square.T
    pack(0, DSQUARE, square)
    send(0, DSQUARE)
    raw[2] = square
    square = 0.125 * twice + wings
    raw[3] = square + square.T
    stat_all(1, groups - 1).wait_recv()
    stats = merged(1, groups)
    energy = stats[:, 0:1] / (n * b)
    bound = jnp.maximum(stats[:, 1:2] - energy, energy + stats[:, 2:3]) + 1e-6
    inverse = 1.0 / bound
    second = inverse * inverse

    g = (energy - level) * inverse
    node = (jnp.where(eye, energy, 0.0) - ham_ref[0, 1]) * inverse
    dnode = -pert_ref[0, 1] * inverse
    state[0, 0] = node
    state[1, 0] = dnode
    put(D, 2.0 * node)
    put(DD, 2.0 * dnode)
    for q in (0, 1):
        edge, dedge = -ham_ref[0, place[q]] * inverse, -pert_ref[0, place[q]] * inverse
        state[0, 1 + q] = edge
        state[1, 1 + q] = dedge
        put(E[q], edge)
        put(DE[q], dedge)
    put(A, raw[0] * second + (4.0 * g) * node - jnp.where(eye, 2.0 * g * g, 0.0))
    put(T, raw[1] * second + g * node - jnp.where(eye, 0.5 * g * g, 0.0))
    put(DA, raw[2] * second + (4.0 * g) * dnode)
    put(DT, raw[3] * second + g * dnode)

    def iterate(step, first, last):
        def pick(yes, no):
            return no if first is False else jnp.where(first, yes, no)

        def shift(q):
            return (energy - inbox[0, SQUARE, q, 2 * h + 1 : 2 * h + 2, 0:1]) * inverse

        for q in (0, 1):
            arrived(step, DIAG, q)
            other = unpack(step, DIAG, q)
            if first is not False:
                other = other * pick(-inverse, 1.0) + jnp.where(eye, pick(energy * inverse, 0.0), 0.0)
            near[0, q] = other
            put(DN[q], other)
            put(F[q], total((E[q], DN[q])))
        node = 1.5 * state[0, 0] - 0.5 * sym(
            total((D, T), turned=((F[0], E[0]), (F[1], E[1])))
        )
        if last:
            dens_ref[0, 1] = jnp.where(eye, 0.5, 0.0) - 0.5 * node
        else:
            state[0, 0] = node
            pack(step + 1, DIAG, node)
            send_late(step + 1, DIAG)
        for q in (0, 1):
            partial[0, q] = total((A, E[q]), (D, F[q]))

        for q in (0, 1):
            v = total((DE[q], DN[q]))
            arrived(step, DDIAG, q)
            other = unpack(step, DDIAG, q)
            if first is not False:
                other = other * pick(-inverse, 1.0)
            near[1, q] = other
            put(DDN[q], other)
            u = total((E[q], DDN[q]))
            put(U[q], u + v)
            put(V[q], u + 2.0 * v)
        dnode = 1.5 * state[1, 0] - 0.5 * sym(
            total((DD, T), (D, DT), turned=((V[0], E[0]), (V[1], E[1])))
        )
        if last:
            resp_ref[0, 1] = (-0.5 * bound) * dnode
        else:
            state[1, 0] = dnode
            pack(step + 1, DDIAG, dnode)
            send_late(step + 1, DDIAG)
        for q in (0, 1):
            partial[1, q] = total((DA, E[q]), (A, DE[q]), (DD, F[q]), (D, U[q]))

        for q in (0, 1):
            arrived(step, SQUARE, q)
            other = unpack(step, SQUARE, q)
            if first is not False:
                g = shift(q)
                other = (
                    other * pick(second, 1.0)
                    + pick(4.0 * g, 0.0) * near[0, q]
                    - jnp.where(eye, pick(2.0 * g * g, 0.0), 0.0)
                )
            put(AN[q], other)
            edge = 1.5 * state[0, 1 + q] - 0.25 * (partial[0, q] + total((E[q], AN[q])))
            if last:
                dens_ref[0, place[q]] = -0.5 * edge
            else:
                state[0, 1 + q] = edge
                put(NEW[q], edge)
        if not last:
            put(D, 2.0 * state[0, 0])
            twice = total((D, D))
            wings = total(turned=((NEW[0], NEW[0]), (NEW[1], NEW[1])))
            square = 0.5 * twice + wings
            pack(step + 1, SQUARE, square)
            send_late(step + 1, SQUARE)
            put(A, square)
            put(T, 0.125 * twice + wings)
        for q in (0, 1):
            partial[1, q] += total((DE[q], AN[q]))

        if last:
            resp_ref[0, place[1]] = (-0.5 * bound) * (1.5 * state[1, 2] - 0.25 * partial[1, 1])
            edge_ref[0], edge_ref[1] = halves((0.125 * bound) * state[0, 2])
        for q in (0, 1):
            arrived(step, DSQUARE, q)
            if last and q == 1:
                late_ref[...] = inbox[step, DSQUARE, 1, 0 : 2 * h + 1]
                continue
            other = unpack(step, DSQUARE, q)
            if first is not False:
                other = other * pick(second, 1.0) + pick(4.0 * shift(q), 0.0) * near[1, q]
            put(DAN[q], other)
            dedge = 1.5 * state[1, 1 + q] - 0.25 * (partial[1, q] + total((E[q], DAN[q])))
            if last:
                resp_ref[0, place[q]] = (-0.5 * bound) * dedge
            else:
                state[1, 1 + q] = dedge
                put(DE[q], dedge)
        if not last:
            put(DD, 2.0 * state[1, 0])
            for q in (0, 1):
                split[E[q]] = split[NEW[q]]
            twice = total((D, DD))
            wings = total(turned=((E[0], DE[0]), (E[1], DE[1])))
            square = 0.5 * twice + wings
            square = square + square.T
            pack(step + 1, DSQUARE, square)
            send_late(step + 1, DSQUARE)
            put(DA, square)
            square = 0.125 * twice + wings
            put(DT, square + square.T)

    @pl.loop(0, ITERS - 1)
    def _(step):
        iterate(step, step == 0, False)

    iterate(ITERS - 1, False, True)

    stat_all(0, GROUP - 1).wait_send()
    stat_all(1, groups - 1).wait_send()
    for step in range(ITERS):
        for kind in range(4):
            for q in (0, 1):
                copy(step, kind, q).wait_send()


def store(dens_ref, resp_ref, edge_ref, late_ref, dens_hbm, resp_hbm, done, sem):
    late = 2 * lax.rem(lax.axis_index("chain"), 2)
    moves = [pltpu.make_async_copy(dens_ref.at[0, k], dens_hbm.at[0, k], sem.at[k]) for k in range(3)]
    for at, k in ((3, 1), (4, 2 - late)):
        moves.append(pltpu.make_async_copy(resp_ref.at[0, k], resp_hbm.at[0, k], sem.at[at]))
    for move in moves:
        move.start()
    high, low = halves(whole(late_ref))
    out = resp_ref[0, late]
    for a, c in ((edge_ref[0], high), (edge_ref[0], low), (edge_ref[1], high)):
        out += jnp.dot(a, c, preferred_element_type=F32)
    done[...] = out
    moves.append(pltpu.make_async_copy(done, resp_hbm.at[0, late], sem.at[5]))
    moves[-1].start()
    for move in moves:
        move.wait()


def per_device(n, ham, pert):
    b = ham.shape[-1]
    packed = (b + 8, b // 2)
    count = max(GROUP, n // GROUP)
    out = pl.pallas_call(
        functools.partial(kernel, n),
        out_shape=(
            jax.ShapeDtypeStruct(ham.shape, F32),
            jax.ShapeDtypeStruct(ham.shape, F32),
            jax.ShapeDtypeStruct((2, b, b), BF16),
            jax.ShapeDtypeStruct((b + 1, b // 2), F32),
        ),
        in_specs=[pl.BlockSpec(memory_space=pltpu.HBM)] * 2,
        out_specs=[pl.BlockSpec(memory_space=pltpu.VMEM)] * 4,
        scratch_shapes=[
            pltpu.VMEM(ham.shape, F32),
            pltpu.VMEM(pert.shape, F32),
            pltpu.VMEM((SLOTS, 2, b, b), BF16),
            pltpu.VMEM((2, 3, b, b), F32),
            pltpu.VMEM((2, 2, b, b), F32),
            pltpu.VMEM((4, b, b), F32),
            pltpu.VMEM((2, 2, b, b), F32),
            pltpu.VMEM((ITERS, 4) + packed, F32),
            pltpu.VMEM((ITERS, 4, 2) + packed, F32),
            pltpu.VMEM((2, 1, 128), F32),
            pltpu.VMEM((2, count, 1, 128), F32),
            pltpu.SemaphoreType.DMA((2, 3)),
            pltpu.SemaphoreType.DMA((ITERS, 4, 2)),
            pltpu.SemaphoreType.DMA((ITERS, 4, 2)),
            pltpu.SemaphoreType.DMA((2,)),
            pltpu.SemaphoreType.DMA((2,)),
            pltpu.SemaphoreType.REGULAR,
            pltpu.SemaphoreType.REGULAR,
        ],
        compiler_params=pltpu.CompilerParams(
            collective_id=0, has_side_effects=True, vmem_limit_bytes=52 * 1024 * 1024
        ),
    )(ham, pert)
    return pl.pallas_call(
        store,
        out_shape=(jax.ShapeDtypeStruct(ham.shape, F32), jax.ShapeDtypeStruct(ham.shape, F32)),
        in_specs=[pl.BlockSpec(memory_space=pltpu.VMEM)] * 4,
        out_specs=[pl.BlockSpec(memory_space=pltpu.HBM)] * 2,
        scratch_shapes=[pltpu.VMEM((b, b), F32), pltpu.SemaphoreType.DMA((6,))],
        compiler_params=pltpu.CompilerParams(vmem_limit_bytes=4 * 1024 * 1024),
    )(*out)


def solution(mesh):
    n = mesh.shape["chain"]
    spec = P("chain", None, None, None)
    return jax.shard_map(
        functools.partial(per_device, n),
        mesh=mesh,
        in_specs=(spec, spec),
        out_specs=(spec, spec),
        check_vma=False,
    )
```
